256 devices in a mesh: dp: 32 (over x, y, core), owner: 8 (over z).
Axes of the slice: x: 4, y: 4, z: 8, core: 2. Of those that a mesh axis runs over, the one named last changes fastest.
Arguments:
- hidden: bfloat16 [8192, 14336], P('dp'), may hold values from -6 to 6
- grad_out: bfloat16 [8192, 4096], P('dp'), may hold values from -6 to 6
- block_row: int32 [1536], replicated, may hold values from 0 to 111
- block_col: int32 [1536], replicated, may hold values from 0 to 31
- owner_of: int32 [1536, 1], replicated, may hold values from 0 to 7; in each aligned block of 1536 rows (0 to 1535, 1536 to 3071, ...) at most 384 rows name the same one
- master: float32 [8, 384, 128, 128], P('owner', 'dp'), may hold values from -6 to 6
- moment1: float32 [8, 384, 128, 128], P('owner', 'dp'), may hold values from -0.0029296875 to 0.0029296875
- moment2: float32 [8, 384, 128, 128], P('owner', 'dp'), may hold values from 9.934108e-09 to 1.5894572e-07
Outputs:
- updated: float32 [8, 384, 128, 128], P('owner', 'dp')
The draws below stay inside these ranges and needn't reach their ends.
Inputs may be any that keep to these rules, and one draw needn't show every extreme that they name: `owner_of`: each owner index names at most 384 listed blocks, and one of them names exactly 384.
All inputs are finite; a program needn't handle non-finite values.
Results may differ from the reference program's by a relative error of at most 0.0006.
Values may be sent and summed in bfloat16 or wider, within the bound.
A program may use at most 128 MiB of HBM per device.

```python
import math
import jax
import jax.numpy as jnp
import numpy as np
from jax import lax

D = 4096
FF = 14336
BLOCK = 128
TOK_DEV = 256
CAP = 384
TOKENS = 8192
NLIST = 1536
N_DP = 32
N_OWNER = 8


def place_ends(drawn, key, low, top_value):
    longest = drawn.shape.index(max(drawn.shape))
    spots = []
    for shift in (0, 1):
        where = [jax.random.randint(jax.random.fold_in(key, axis), (), 0, length) for axis, length in enumerate(drawn.shape)]
        where[longest] = (where[longest] + shift) % drawn.shape[longest]
        spots.append(tuple(where))
    return drawn.at[spots[0]].set(low).at[spots[1]].set(top_value)


def shard_levels(rng, shape, cuts, low, largest):
    def one(position, shards_of):
        draws = jax.random.uniform(jax.random.fold_in(jax.random.fold_in(rng, 6), position), (shards_of,), jnp.float32, low / len(cuts), largest / len(cuts))
        return jnp.repeat(jnp.exp(draws), shape[position] // shards_of).reshape((-1,) + (1,) * (len(shape) - position - 1))

    level = one(*cuts[0])
    for cut in cuts[1:]:
        level = level * one(*cut)
    return level


def shared_out(stream_key, own, number, rows, count, top, most, lean):
    sequence = jax.random.permutation(stream_key, count)
    crowded, common = shares(count, rows * top, most, lean, True), shares(count, rows * top, most, lean, False)
    places = jnp.arange(count)

    def named(sizes, turn):
        used = int((sizes > 0).sum())
        fixed = max(1, used // 4)
        shifted = fixed + (places - fixed + turn * (used - fixed)) % max(1, count - fixed)
        return jnp.zeros((count,), jnp.int32).at[sequence[jnp.where(places < fixed, places, shifted)]].set(jnp.asarray(sizes, jnp.int32))

    sizes = jnp.where(number % 4 == 0, named(crowded, number // 4), named(common, number - number // 4 - 1))
    mixed = jax.random.permutation(jax.random.fold_in(own, 3), count)
    source_of, receiver = mixed[0:count // 2 * 2:2], mixed[1:count // 2 * 2:2]
    margin = jnp.minimum(sizes[source_of] - 1, most - sizes[receiver]) // 2
    margin = jnp.where((source_of == sequence[0]) | (receiver == sequence[0]) | (sizes[receiver] == 0), 0, jnp.maximum(margin, 0))
    shifted = jax.random.randint(jax.random.fold_in(own, 4), (count // 2,), 0, 1 << 20) % (margin + 1)
    sizes = sizes.at[source_of].add(-shifted).at[receiver].add(shifted)
    items = jnp.searchsorted(jnp.cumsum(sizes), jnp.arange(rows * top), side="right").astype(jnp.int32)
    listing = items.reshape(top, rows).T
    listing = listing[jax.random.permutation(jax.random.fold_in(own, 1), rows)]
    turn = jax.random.randint(jax.random.fold_in(own, 2), (rows, 1), 0, top)
    return jnp.take_along_axis(listing, (jnp.arange(top)[None, :] + turn) % top, axis=1)


def shares(count, total, bound, lean, full):
    loads = [(1 << 20) // math.isqrt(standing ** lean) + 1 for standing in range(1, count + 1)]
    largest = bound if full else min(bound, max(-(-total // count), total * loads[0] // sum(loads)))
    least = 1 if total - largest >= count - 1 else 0
    given, surplus = [largest] + [least] * (count - 1), total - largest - least * (count - 1)
    while surplus > 0:
        free = [i for i in range(1, count) if given[i] < largest] or [i for i in range(1, count) if given[i] < bound]
        pool, remaining = sum([loads[i] for i in free]), surplus
        for i in free:
            extra = min(bound - given[i], max(1, remaining * loads[i] // pool), surplus)
            given[i] = given[i] + extra
            surplus = surplus - extra
    return np.array(given)


def normal_values(own_key, extent, width, limit, shards=(), held_as=jnp.bfloat16):
    level = shard_levels(own_key, extent, shards, -0.22, 0.18) if shards else 1.0
    result = jax.random.normal(own_key, extent, jnp.float32) * width * level
    return jnp.minimum(jnp.maximum(result, -limit), limit).astype(held_as)


def setup_inputs(seed: int = 0) -> dict:
    splits = jax.random.split(jax.random.key(seed), 9)
    hidden = normal_values(splits[0], (TOKENS, FF), 1.0, 6.0, ((0, 32),))
    grad_out = normal_values(splits[1], (TOKENS, D), 1.0, 6.0, ((0, 32),))
    block_row = place_ends(jax.random.randint(splits[2], (NLIST,), 0, FF // BLOCK), jax.random.fold_in(splits[2], 1), 0, (FF // BLOCK) - 1).astype(jnp.int32)
    block_col = place_ends(jax.random.randint(splits[3], (NLIST,), 0, D // BLOCK), jax.random.fold_in(splits[3], 1), 0, (D // BLOCK) - 1).astype(jnp.int32)
    owner_of_keys = jax.random.split(jax.random.fold_in(splits[4], 1), NLIST // NLIST)
    owner_of_turns = jax.random.permutation(jax.random.fold_in(splits[4], 3), NLIST // NLIST)
    owner_of = jax.vmap(lambda own, number: shared_out(jax.random.fold_in(splits[4], 2), own, number, NLIST, N_OWNER, 1, CAP, 2))(owner_of_keys, owner_of_turns).reshape((NLIST, 1))
    master = normal_values(splits[5], (N_OWNER, CAP, BLOCK, BLOCK), 1.0, 6.0, ((0, 8), (1, 32)), jnp.float32)
    moment1 = normal_values(splits[6], (N_OWNER, CAP, BLOCK, BLOCK), ((NLIST * BLOCK * BLOCK) ** -0.5), 0.0029296875, ((0, 8), (1, 32)), jnp.float32)
    moment2 = jnp.clip(jnp.exp(math.log(1.5894572413799324e-07) - 2.7725887 * jax.random.uniform(splits[7], (N_OWNER, CAP, BLOCK, BLOCK), jnp.float32) ** shard_levels(splits[7], (N_OWNER, CAP, BLOCK, BLOCK), ((0, 8), (1, 32)), -0.2, 0.2)), 9.934107758624577e-09, 1.5894572413799324e-07)
    return {"hidden": hidden, "grad_out": grad_out, "block_row": block_row, "block_col": block_col, "owner_of": owner_of, "master": master, "moment1": moment1, "moment2": moment2}


def reference(hidden, grad_out, block_row, block_col, owner_of, master, moment1, moment2):
    hidden_four = hidden.reshape(N_DP, TOK_DEV, FF // BLOCK, BLOCK).astype(jnp.float32)
    grad_four = grad_out.reshape(N_DP, TOK_DEV, D // BLOCK, BLOCK).astype(jnp.float32)
    group = math.gcd(NLIST, 64)

    def one_group(pair):
        rows_now, cols_now = pair
        left = jnp.take(hidden_four, rows_now, axis=2)
        right = jnp.take(grad_four, cols_now, axis=2)
        parts = jnp.einsum('ntgi,ntgj->ngij', left, right)
        parts = lax.optimization_barrier(parts.astype(jnp.bfloat16)).astype(jnp.float32)
        return lax.optimization_barrier(jnp.sum(parts, axis=0))
    grads = lax.map(one_group, (block_row.reshape(-1, group), block_col.reshape(-1, group)))
    grads = grads.reshape(NLIST, BLOCK * BLOCK)
    owners = owner_of[:, 0]
    onehot = (owners[:, None] == jnp.arange(N_OWNER, dtype=jnp.int32)[None, :]).astype(jnp.int32)
    ranks = lax.optimization_barrier(jnp.sum((jnp.cumsum(onehot, axis=0) - 1) * onehot, axis=1)).astype(jnp.int32)
    slot_key = owners * CAP + ranks
    select = (jnp.arange(N_OWNER * CAP, dtype=jnp.int32)[:, None] == slot_key[None, :]).astype(jnp.float32)
    slot_grad = jnp.dot(select, grads, precision=lax.Precision.HIGHEST).reshape(N_OWNER, CAP, BLOCK, BLOCK)
    total = jnp.sum(slot_grad * slot_grad)
    clip = 1.0 / jnp.maximum(jnp.sqrt(total), 1.0)
    scaled = clip * slot_grad
    first = 0.9 * moment1 + 0.1 * scaled
    second = 0.95 * moment2 + 0.05 * scaled * scaled
    direction = first / (1.0 - 0.9 ** 10) / (jnp.sqrt(second / (1.0 - 0.95 ** 10)) + 1e-08)
    return master - 0.25 * (direction + 0.1 * master)
```

```python
import functools

import jax
import jax.numpy as jnp
from jax import lax
from jax.experimental import pallas as pl
from jax.experimental.pallas import tpu as pltpu
from jax.sharding import PartitionSpec as P

BLOCK = 128
CAP = 384
N_OWNER = 8
MESH = pl.DeviceIdType.MESH
PAIR, XA, XB0, XB1, YA, YB0, YB1 = 0, 1, 3, 5, 7, 9, 11


def slot_table(owner_of, block_row, block_col, me_index, capacity):
    owned = (owner_of[:, 0] == me_index).astype(jnp.int32)
    ranks = jnp.cumsum(owned) - 1
    slots = jnp.arange(capacity, dtype=jnp.int32)
    match = (owned[None, :] == 1) & (ranks[None, :] == slots[:, None])
    live = jnp.any(match, axis=1).astype(jnp.float32)
    slot_rows = jnp.sum(jnp.where(match, block_row[None, :], 0), axis=1)
    slot_cols = jnp.sum(jnp.where(match, block_col[None, :], 0), axis=1)
    return (slot_rows, slot_cols, live)


def wrap(value, size):
    return lax.rem(value, size)


def kernel(items, row_ref, col_ref, live_ref, hidden_hbm, grad_hbm, slot_grad_ref, total_ref,
           hidden, grad, grad_t, to_pair, from_pair, chip, ring_a, ring_b, line, last_a, last_b,
           sums, sum_in, load_sem, send_sem, recv_sem, sum_send, sum_recv):
    f32, bf16 = jnp.float32, jnp.bfloat16
    d = lax.axis_index("dp")
    z = lax.axis_index("owner")
    x, y, c = lax.div(d, 8), wrap(lax.div(d, 2), 4), wrap(d, 2)

    def device(px, py, pc):
        return {"dp": (px * 4 + py) * 2 + pc}

    partner = device(x, y, 1 - c)

    def near(axis, step):
        if axis == 0:
            return device(wrap(x + step, 4), y, c)
        return device(x, wrap(y + step, 4), c)

    def up(step):
        return {"owner": wrap(z + step, N_OWNER)}

    def load(src, dst, sem):
        def body(k, carry):
            columns = pl.ds(pl.multiple_of(k * BLOCK, BLOCK), BLOCK)
            pltpu.make_async_copy(src.at[:, columns], dst.at[k], sem).start()
            return carry
        lax.fori_loop(0, dst.shape[0], body, 0)

    load(grad_hbm, grad, load_sem.at[0])
    load(hidden_hbm, hidden, load_sem.at[1])

    groups = [[partner], [near(0, k) for k in (1, 2, 3)], [near(1, k) for k in (1, 2, 3)],
              [up(k) for k in range(1, N_OWNER)]]
    barrier = pltpu.get_barrier_semaphore()
    everyone = [who for group in groups for who in group]
    for who in everyone:
        pl.semaphore_signal(barrier, inc=1, device_id=who, device_id_type=MESH)

    pltpu.make_async_copy(grad, grad, load_sem.at[0]).wait()

    def turn(k, carry):
        grad_t[k] = grad[k].T
        return carry

    lax.fori_loop(0, grad_t.shape[0], turn, 0)
    pltpu.make_async_copy(hidden, hidden, load_sem.at[1]).wait()
    pl.semaphore_wait(barrier, len(everyone))

    started = []

    def send(src, dst, item, kind, who):
        copy = pltpu.make_async_remote_copy(
            src_ref=src, dst_ref=dst, send_sem=send_sem.at[item, kind],
            recv_sem=recv_sem.at[item, kind], device_id=who, device_id_type=MESH)
        copy.start()
        started.append(copy)
        arrivals[item, kind] = copy

    arrivals = {}

    def arrive(item, kind):
        arrivals[item, kind].wait_recv()

    def product(slot):
        row, col = row_ref[slot], col_ref[slot]
        return jnp.dot(grad_t[col], hidden[row], preferred_element_type=f32)

    def slot_of(item, ra, rb, core):
        if item % 2 == 0:
            px, py = wrap(x + ra, 4), wrap(y + rb, 4)
        else:
            px, py = wrap(x + rb, 4), wrap(y + ra, 4)
        return ((px * 4 + py) * 2 + core) * items + item

    def partner_products(item):
        def body(ra, carry):
            for rb in range(4):
                to_pair[item, ra * 4 + rb] = product(slot_of(item, ra, rb, 1 - c)).astype(bf16)
            return carry
        lax.fori_loop(0, 4, body, 0)
        send(to_pair.at[item], from_pair.at[item], item, PAIR, partner)

    def own_products(item):
        arrive(item, PAIR)

        def body(ra, carry):
            for rb in range(4):
                j = ra * 4 + rb
                value = product(slot_of(item, ra, rb, c)) + from_pair[item, j].astype(f32)
                chip[item, j] = value.astype(bf16)
            return carry
        lax.fori_loop(0, 4, body, 0)
        axis = item % 2
        send(chip.at[item, pl.ds(8, 2)], ring_a.at[item, 0], item, XA, near(axis, 1))
        send(chip.at[item, pl.ds(10, 2)], ring_a.at[item, 1], item, XA + 1, near(axis, 3))
        send(chip.at[item, pl.ds(6, 2)], ring_b.at[item, 0, pl.ds(2, 2)], item, XB0, near(axis, 1))
        send(chip.at[item, pl.ds(12, 2)], ring_b.at[item, 1, pl.ds(0, 2)], item, XB0 + 1, near(axis, 3))

    def ring_step(item):
        axis = item % 2
        arrive(item, XA)
        chip[item, 4:6] = (chip[item, 4:6].astype(f32) + ring_a[item, 0].astype(f32)).astype(bf16)
        send(chip.at[item, pl.ds(4, 2)], ring_b.at[item, 0, pl.ds(0, 2)], item, XB1, near(axis, 1))
        arrive(item, XA + 1)
        chip[item, 14:16] = (chip[item, 14:16].astype(f32) + ring_a[item, 1].astype(f32)).astype(bf16)
        send(chip.at[item, pl.ds(14, 2)], ring_b.at[item, 1, pl.ds(2, 2)], item, XB1 + 1, near(axis, 3))

    def ring_end(item):
        axis = 1 - item % 2
        for kind in (XB0, XB0 + 1, XB1, XB1 + 1):
            arrive(item, kind)
        for rb in (2, 1, 3, 0):
            value = (chip[item, rb].astype(f32) + ring_b[item, 0, rb].astype(f32)
                     + ring_b[item, 1, rb].astype(f32))
            line[item, rb] = value.astype(bf16)
        half = BLOCK // 2
        low, high = pl.ds(0, half), pl.ds(half, half)
        send(line.at[item, 2, low], last_a.at[item, 0], item, YA, near(axis, 1))
        send(line.at[item, 2, high], last_a.at[item, 1], item, YA + 1, near(axis, 3))
        send(line.at[item, 1, high], last_b.at[item, 0, high], item, YB0, near(axis, 1))
        send(line.at[item, 3, low], last_b.at[item, 1, low], item, YB0 + 1, near(axis, 3))

    def line_step(item):
        axis = 1 - item % 2
        half = BLOCK // 2
        low, high = pl.ds(0, half), pl.ds(half, half)
        arrive(item, YA)
        line[item, 1, :half] = (line[item, 1, :half].astype(f32) + last_a[item, 0].astype(f32)).astype(bf16)
        send(line.at[item, 1, low], last_b.at[item, 0, low], item, YB1, near(axis, 1))
        arrive(item, YA + 1)
        line[item, 3, half:] = (line[item, 3, half:].astype(f32) + last_a[item, 1].astype(f32)).astype(bf16)
        send(line.at[item, 3, high], last_b.at[item, 1, high], item, YB1 + 1, near(axis, 3))

    def finish(item):
        for kind in (YB0, YB0 + 1, YB1, YB1 + 1):
            arrive(item, kind)
        value = (line[item, 0].astype(f32) + last_b[item, 0].astype(f32) + last_b[item, 1].astype(f32))
        value = value * live_ref[d * items + item]
        slot_grad_ref[item] = value.T
        return jnp.sum((value * value).reshape(-1, 8, BLOCK), axis=0)

    steps = items // 2
    part = jnp.zeros((8, BLOCK), f32)
    both = lambda stage, step: [stage(2 * step + q) for q in (0, 1)] if 0 <= step < steps else []
    for tick in range(-1, steps + 4):
        both(partner_products, tick + 1)
        both(own_products, tick)
        both(ring_step, tick - 1)
        both(line_step, tick - 3)
        both(ring_end, tick - 2)
        for piece in both(finish, tick - 4):
            part = part + piece

    sums[0] = part
    first = 0
    for n, group in enumerate(groups):
        for k, who in enumerate(group):
            copy = pltpu.make_async_remote_copy(
                src_ref=sums.at[n], dst_ref=sum_in.at[first + k], send_sem=sum_send.at[first + k],
                recv_sem=sum_recv.at[first + k], device_id=who, device_id_type=MESH)
            copy.start()
            started.append(copy)
        for k, copy in enumerate(started[-len(group):]):
            copy.wait_recv()
            part = part + sum_in[first + k]
        first += len(group)
        if n + 1 < len(groups):
            sums[n + 1] = part
    total_ref[...] = part
    for copy in started:
        copy.wait_send()


def reduce_blocks(rows, cols, live, hidden, grad_out, items):
    tokens, features = hidden.shape[0], grad_out.shape[1]
    bf16, f32 = jnp.bfloat16, jnp.float32
    peers = 1 + 3 + 3 + N_OWNER - 1
    block = (BLOCK, BLOCK)
    smem = pl.BlockSpec(memory_space=pltpu.SMEM)
    vmem = pl.BlockSpec(memory_space=pltpu.VMEM)
    hbm = pl.BlockSpec(memory_space=pl.ANY)
    return pl.pallas_call(
        functools.partial(kernel, items),
        out_shape=(jax.ShapeDtypeStruct((items, *block), f32), jax.ShapeDtypeStruct((8, BLOCK), f32)),
        in_specs=[smem, smem, smem, hbm, hbm],
        out_specs=(vmem, vmem),
        scratch_shapes=[
            pltpu.VMEM((hidden.shape[1] // BLOCK, tokens, BLOCK), bf16),
            pltpu.VMEM((features // BLOCK, tokens, BLOCK), bf16),
            pltpu.VMEM((features // BLOCK, BLOCK, tokens), bf16),
            pltpu.VMEM((items, 16, *block), bf16),
            pltpu.VMEM((items, 16, *block), bf16),
            pltpu.VMEM((items, 16, *block), bf16),
            pltpu.VMEM((items, 2, 2, *block), bf16),
            pltpu.VMEM((items, 2, 4, *block), bf16),
            pltpu.VMEM((items, 4, *block), bf16),
            pltpu.VMEM((items, 2, BLOCK // 2, BLOCK), bf16),
            pltpu.VMEM((items, 2, *block), bf16),
            pltpu.VMEM((4, 8, BLOCK), f32),
            pltpu.VMEM((peers, 8, BLOCK), f32),
            pltpu.SemaphoreType.DMA((2,)),
            pltpu.SemaphoreType.DMA((items, 13)),
            pltpu.SemaphoreType.DMA((items, 13)),
            pltpu.SemaphoreType.DMA((peers,)),
            pltpu.SemaphoreType.DMA((peers,)),
        ],
        compiler_params=pltpu.CompilerParams(
            collective_id=0, has_side_effects=True, vmem_limit_bytes=62 * 1024 * 1024),
        name="reduce_blocks",
    )(rows, cols, live, hidden, grad_out)


def on_device(hidden, grad_out, block_row, block_col, owner_of, master, moment1, moment2):
    share = master.shape[1]
    me_index = lax.axis_index("owner")
    rows, cols, live = slot_table(owner_of, block_row, block_col, me_index, CAP)
    shares, parts = reduce_blocks(rows, cols, live, hidden, grad_out, share)
    total = jnp.sum(parts)
    clip = 1.0 / jnp.maximum(jnp.sqrt(total), 1.0)
    scaled = clip * shares[None]
    first = 0.9 * moment1 + 0.1 * scaled
    second = 0.95 * moment2 + 0.05 * scaled * scaled
    direction = first / (1.0 - 0.9**10) / (jnp.sqrt(second / (1.0 - 0.95**10)) + 1e-08)
    return master - 0.25 * (direction + 0.1 * master)


def solution(mesh):
    placed = (
        P("dp", None),
        P("dp", None),
        P(),
        P(),
        P(),
        P("owner", "dp", None, None),
        P("owner", "dp", None, None),
        P("owner", "dp", None, None),
    )
    return jax.shard_map(
        on_device,
        mesh=mesh,
        in_specs=placed,
        out_specs=P("owner", "dp", None, None),
        check_vma=False,
    )
```

```python
import functools

import jax
import jax.numpy as jnp
from jax import lax
from jax.experimental import pallas as pl
from jax.experimental.pallas import tpu as pltpu
from jax.sharding import PartitionSpec as P

BLOCK = 128
N_OWNER = 8
MESH = pl.DeviceIdType.MESH
CHUNKS = 3
CHIPS = 16
PAIR, XA, XB0, XB1, YA, YB0, YB1 = 0, 1, 3, 5, 7, 9, 11


def sorted_places(owner_of, block_row, block_col, plane):
    owners = jnp.arange(N_OWNER, dtype=jnp.int32)
    named = (owner_of[:, 0][None, :] == owners[:, None]).astype(jnp.int32)
    running = jnp.cumsum(named, axis=1)
    counts = running[:, -1]
    starts = jnp.sum(jnp.where(owners[None, :] < owners[:, None], counts[None, :], 0), axis=1)
    spot = jnp.sum(named * (running - 1 + starts[:, None]), axis=0)
    place = jnp.arange(CHUNKS * 4 * CHIPS, dtype=jnp.int32)
    chunk, pos, chip = place // (4 * CHIPS), (place // CHIPS) % 4, place % CHIPS
    wanted = CHIPS * (24 * pos + CHUNKS * plane + chunk) + chip
    packed = block_row * 32 + block_col
    listed = jnp.sum(jnp.where(wanted[:, None] == spot[None, :], packed[None, :], 0), axis=1)
    return listed, starts, counts


def wrap(value, size):
    return lax.rem(value, size)


def kernel(items, share, place_ref, start_ref, count_ref, hidden_hbm, grad_hbm, slot_grad_ref, total_ref,
           hidden, grad, grad_t, to_pair, from_pair, chip, ring_a, ring_b, line, last_a, last_b,
           done_0, done_1, done_2, to_owner, gathered, to_slot, landed,
           sums, sum_in, load_sem, send_sem, recv_sem, move_send, move_recv, sum_send, sum_recv):
    f32, bf16 = jnp.float32, jnp.bfloat16
    d = lax.axis_index("dp")
    z = lax.axis_index("owner")
    x, y, c = lax.div(d, 8), wrap(lax.div(d, 2), 4), wrap(d, 2)

    def device(px, py, pc):
        return {"dp": (px * 4 + py) * 2 + pc}

    partner = device(x, y, 1 - c)

    def near(axis, step):
        if axis == 0:
            return device(wrap(x + step, 4), y, c)
        return device(x, wrap(y + step, 4), c)

    def up(step):
        return {"owner": wrap(z + step, N_OWNER)}

    def load(src, dst, sem):
        def body(k, carry):
            columns = pl.ds(pl.multiple_of(k * BLOCK, BLOCK), BLOCK)
            pltpu.make_async_copy(src.at[:, columns], dst.at[k], sem).start()
            return carry
        lax.fori_loop(0, dst.shape[0], body, 0)

    load(grad_hbm, grad, load_sem.at[0])
    load(hidden_hbm, hidden, load_sem.at[1])

    groups = [[partner], [near(0, k) for k in (1, 2, 3)], [near(1, k) for k in (1, 2, 3)],
              [up(k) for k in range(1, N_OWNER)]]
    barrier = pltpu.get_barrier_semaphore()
    offsets = [(dx, dy) for dx in range(4) for dy in range(4) if dx or dy]
    spread = [device(wrap(x + dx, 4), wrap(y + dy, 4), c) for dx, dy in offsets]
    everyone = [partner] + spread + groups[3]
    for who in everyone:
        pl.semaphore_signal(barrier, inc=1, device_id=who, device_id_type=MESH)

    pltpu.make_async_copy(grad, grad, load_sem.at[0]).wait()

    def turn(k, carry):
        grad_t[k] = grad[k].T
        return carry

    lax.fori_loop(0, grad_t.shape[0], turn, 0)
    pltpu.make_async_copy(hidden, hidden, load_sem.at[1]).wait()

    started = []

    def send(src, dst, item, kind, who):
        copy = pltpu.make_async_remote_copy(
            src_ref=src, dst_ref=dst, send_sem=send_sem.at[item, kind],
            recv_sem=recv_sem.at[item, kind], device_id=who, device_id_type=MESH)
        copy.start()
        started.append(copy)
        arrivals[item, kind] = copy

    arrivals = {}

    def arrive(item, kind):
        arrivals[item, kind].wait_recv()

    def product(place):
        both_indices = place_ref[place]
        row, col = lax.shift_right_logical(both_indices, 5), both_indices & 31
        return jnp.dot(grad_t[col], hidden[row], preferred_element_type=f32)

    def slot_of(item, ra, rb, core):
        if item % 2 == 0:
            px, py = wrap(x + ra, 4), wrap(y + rb, 4)
        else:
            px, py = wrap(x + rb, 4), wrap(y + ra, 4)
        return ((item // 2) * 4 + 2 * core + item % 2) * CHIPS + px * 4 + py

    def partner_products(item):
        def body(ra, carry):
            for rb in range(4):
                to_pair[item, ra * 4 + rb] = product(slot_of(item, ra, rb, 1 - c)).astype(bf16)
            return carry
        lax.fori_loop(0, 4, body, 0)
        if item == 0:
            pl.semaphore_wait(barrier, len(everyone))
        send(to_pair.at[item], from_pair.at[item], item, PAIR, partner)

    def own_products(item):
        arrive(item, PAIR)

        def body(ra, carry):
            for rb in range(4):
                j = ra * 4 + rb
                value = product(slot_of(item, ra, rb, c)) + from_pair[item, j].astype(f32)
                chip[item, j] = value.astype(bf16)
            return carry
        lax.fori_loop(0, 4, body, 0)
        axis = item % 2
        send(chip.at[item, pl.ds(8, 2)], ring_a.at[item, 0], item, XA, near(axis, 1))
        send(chip.at[item, pl.ds(10, 2)], ring_a.at[item, 1], item, XA + 1, near(axis, 3))
        send(chip.at[item, pl.ds(6, 2)], ring_b.at[item, 0, pl.ds(2, 2)], item, XB0, near(axis, 1))
        send(chip.at[item, pl.ds(12, 2)], ring_b.at[item, 1, pl.ds(0, 2)], item, XB0 + 1, near(axis, 3))

    def ring_step(item):
        axis = item % 2
        arrive(item, XA)
        chip[item, 4:6] = (chip[item, 4:6].astype(f32) + ring_a[item, 0].astype(f32)).astype(bf16)
        send(chip.at[item, pl.ds(4, 2)], ring_b.at[item, 0, pl.ds(0, 2)], item, XB1, near(axis, 1))
        arrive(item, XA + 1)
        chip[item, 14:16] = (chip[item, 14:16].astype(f32) + ring_a[item, 1].astype(f32)).astype(bf16)
        send(chip.at[item, pl.ds(14, 2)], ring_b.at[item, 1, pl.ds(2, 2)], item, XB1 + 1, near(axis, 3))

    def ring_end(item):
        axis = 1 - item % 2
        for kind in (XB0, XB0 + 1, XB1, XB1 + 1):
            arrive(item, kind)
        for rb in (2, 1, 3, 0):
            value = (chip[item, rb].astype(f32) + ring_b[item, 0, rb].astype(f32)
                     + ring_b[item, 1, rb].astype(f32))
            line[item, rb] = value.astype(bf16)
        half = BLOCK // 2
        low, high = pl.ds(0, half), pl.ds(half, half)
        send(line.at[item, 2, low], last_a.at[item, 0], item, YA, near(axis, 1))
        send(line.at[item, 2, high], last_a.at[item, 1], item, YA + 1, near(axis, 3))
        send(line.at[item, 1, high], last_b.at[item, 0, high], item, YB0, near(axis, 1))
        send(line.at[item, 3, low], last_b.at[item, 1, low], item, YB0 + 1, near(axis, 3))

    def line_step(item):
        axis = 1 - item % 2
        half = BLOCK // 2
        low, high = pl.ds(0, half), pl.ds(half, half)
        arrive(item, YA)
        line[item, 1, :half] = (line[item, 1, :half].astype(f32) + last_a[item, 0].astype(f32)).astype(bf16)
        send(line.at[item, 1, low], last_b.at[item, 0, low], item, YB1, near(axis, 1))
        arrive(item, YA + 1)
        line[item, 3, half:] = (line[item, 3, half:].astype(f32) + last_a[item, 1].astype(f32)).astype(bf16)
        send(line.at[item, 3, high], last_b.at[item, 1, high], item, YB1 + 1, near(axis, 3))

    def finish(item):
        for kind in (YB0, YB0 + 1, YB1, YB1 + 1):
            arrive(item, kind)
        value = (line[item, 0].astype(f32) + last_b[item, 0].astype(f32) + last_b[item, 1].astype(f32))
        done[item // 2][c * 2 + item % 2] = value.astype(bf16)
        return jnp.sum((value * value).reshape(-1, 8, BLOCK), axis=0)

    done = (done_0, done_1, done_2)
    me_chip = x * 4 + y
    half = BLOCK // 2
    mine = pl.ds(pl.multiple_of(c * half, half), half)
    moves = {}

    def move(src, dst, index, who):
        copy = pltpu.make_async_remote_copy(
            src_ref=src, dst_ref=dst, send_sem=move_send.at[index], recv_sem=move_recv.at[index],
            device_id=who, device_id_type=MESH)
        copy.start()
        started.append(copy)
        moves[index] = copy

    def share_done(chunk):
        move(done[chunk].at[pl.ds(2 * c, 2)], done[chunk].at[pl.ds(2 * c, 2)], chunk, partner)

    def held_for(chunk, owner):
        first = start_ref[owner] - me_chip - CHIPS * (CHUNKS * z + chunk) + 383
        pos = jnp.minimum(lax.div(jnp.maximum(first, 0), 384), 3)
        return done[chunk][pos]

    def to_owners(chunk):
        moves[chunk].wait_recv()
        base = 3 + 6 * chunk
        for j in (1, 2, 0):
            owner = wrap(z + 2 * j + 1 + c, N_OWNER)
            to_owner[chunk, j] = held_for(chunk, owner)
            move(to_owner.at[chunk, j], gathered.at[chunk * 8 + c * 3 + j], base + j, {"owner": owner})
        owner = wrap(z + 7, N_OWNER)
        to_owner[chunk, 3] = held_for(chunk, owner)
        move(to_owner.at[chunk, 3, mine], gathered.at[chunk * 8 + 6, mine], base + 3, {"owner": owner})
        gathered[chunk * 8 + 7] = held_for(chunk, z)

    def share_gathered(chunk):
        base = 3 + 6 * chunk
        for j in range(4):
            moves[base + j].wait_recv()
        trio = gathered.at[pl.ds(chunk * 8 + c * 3, 3)]
        move(trio, trio, base + 4, partner)
        rest = gathered.at[chunk * 8 + 6, mine]
        move(rest, rest, base + 5, partner)

    start, count = start_ref[z], count_ref[z]

    def block_for(to_chip):
        first = start + share * (2 * to_chip + c)
        spot = first + ((me_chip - first) & (CHIPS - 1))
        q = jnp.minimum(lax.div(spot, CHIPS), 95)
        chunk = wrap(q, CHUNKS)
        away = (z - lax.div(q, CHUNKS)) & (N_OWNER - 1)
        index = 3 * ((away + 1) & 1) + lax.shift_right_logical(away + 7, 1) - 4
        index = jnp.where(away == 0, 7, jnp.where(away == 7, 6, index))
        return gathered[chunk * 8 + index]

    def to_slots():
        for chunk in range(CHUNKS):
            moves[3 + 6 * chunk + 4].wait_recv()
            moves[3 + 6 * chunk + 5].wait_recv()
        base = 3 + 6 * CHUNKS
        for k, (dx, dy) in enumerate(offsets):
            to_slot[k] = block_for(wrap(x + dx, 4) * 4 + wrap(y + dy, 4))
            move(to_slot.at[k], landed.at[me_chip], base + k, spread[k])
        landed[me_chip] = block_for(me_chip)

    def store_slots():
        for k in range(len(offsets)):
            moves[3 + 6 * CHUNKS + k].wait_recv()
        for i in range(share):
            slot = d * share + i
            value = landed[(start + slot) & (CHIPS - 1)].astype(f32)
            slot_grad_ref[i] = (value * (slot < count).astype(f32)).T

    def add_start(n, value):
        first = sum(len(group) for group in groups[:n])
        sums[n] = value
        copies = []
        for k, who in enumerate(groups[n]):
            copy = pltpu.make_async_remote_copy(
                src_ref=sums.at[n], dst_ref=sum_in.at[first + k], send_sem=sum_send.at[first + k],
                recv_sem=sum_recv.at[first + k], device_id=who, device_id_type=MESH)
            copy.start()
            started.append(copy)
            copies.append((first + k, copy))
        return copies

    def add_end(value, copies):
        for k, copy in copies:
            copy.wait_recv()
            value = value + sum_in[k]
        return value

    part = jnp.zeros((8, BLOCK), f32)

    def pair(stage, chunk):
        return [stage(2 * chunk), stage(2 * chunk + 1)]

    def close(chunk, value):
        for piece in pair(finish, chunk):
            value = value + piece
        share_done(chunk)
        return value

    pair(partner_products, 0)
    pair(partner_products, 1)
    pair(own_products, 0)
    pair(partner_products, 2)
    pair(own_products, 1)
    pair(ring_step, 0)
    pair(own_products, 2)
    pair(ring_step, 1)
    pair(ring_end, 0)
    pair(ring_step, 2)
    pair(line_step, 0)
    pair(ring_end, 1)
    part = close(0, part)
    pair(ring_end, 2)
    pair(line_step, 1)
    to_owners(0)
    part = close(1, part)
    pair(line_step, 2)
    share_gathered(0)
    to_owners(1)
    part = close(2, part)
    copies = add_start(0, part)
    share_gathered(1)
    to_owners(2)
    part = add_end(part, copies)
    copies = add_start(1, part)
    share_gathered(2)
    part = add_end(part, copies)
    copies = add_start(2, part)
    to_slots()
    part = add_end(part, copies)
    copies = add_start(3, part)
    store_slots()
    part = add_end(part, copies)
    total_ref[0, 0] = jnp.sum(part)
    for copy in started:
        copy.wait_send()


def reduce_blocks(places, starts, counts, hidden, grad_out, share):
    tokens, features = hidden.shape[0], grad_out.shape[1]
    bf16, f32 = jnp.bfloat16, jnp.float32
    items = 2 * CHUNKS
    peers = 1 + 3 + 3 + N_OWNER - 1
    block = (BLOCK, BLOCK)
    smem = pl.BlockSpec(memory_space=pltpu.SMEM)
    vmem = pl.BlockSpec(memory_space=pltpu.VMEM)
    hbm = pl.BlockSpec(memory_space=pl.ANY)
    return pl.pallas_call(
        functools.partial(kernel, items, share),
        out_shape=(jax.ShapeDtypeStruct((share, *block), f32), jax.ShapeDtypeStruct((1, 1), f32)),
        in_specs=[smem, smem, smem, hbm, hbm],
        out_specs=(vmem, smem),
        scratch_shapes=[
            pltpu.VMEM((hidden.shape[1] // BLOCK, tokens, BLOCK), bf16),
            pltpu.VMEM((features // BLOCK, tokens, BLOCK), bf16),
            pltpu.VMEM((features // BLOCK, BLOCK, tokens), bf16),
            pltpu.VMEM((items, 16, *block), bf16),
            pltpu.VMEM((items, 16, *block), bf16),
            pltpu.VMEM((items, 16, *block), bf16),
            pltpu.VMEM((items, 2, 2, *block), bf16),
            pltpu.VMEM((items, 2, 4, *block), bf16),
            pltpu.VMEM((items, 4, *block), bf16),
            pltpu.VMEM((items, 2, BLOCK // 2, BLOCK), bf16),
            pltpu.VMEM((items, 2, *block), bf16),
            pltpu.VMEM((4, *block), bf16),
            pltpu.VMEM((4, *block), bf16),
            pltpu.VMEM((4, *block), bf16),
            pltpu.VMEM((CHUNKS, 4, *block), bf16),
            pltpu.VMEM((CHUNKS * N_OWNER, *block), bf16),
            pltpu.VMEM((CHIPS - 1, *block), bf16),
            pltpu.VMEM((CHIPS, *block), bf16),
            pltpu.VMEM((4, 8, BLOCK), f32),
            pltpu.VMEM((peers, 8, BLOCK), f32),
            pltpu.SemaphoreType.DMA((2,)),
            pltpu.SemaphoreType.DMA((items, 13)),
            pltpu.SemaphoreType.DMA((items, 13)),
            pltpu.SemaphoreType.DMA((7 * CHUNKS + CHIPS - 1,)),
            pltpu.SemaphoreType.DMA((7 * CHUNKS + CHIPS - 1,)),
            pltpu.SemaphoreType.DMA((peers,)),
            pltpu.SemaphoreType.DMA((peers,)),
        ],
        compiler_params=pltpu.CompilerParams(
            collective_id=0, has_side_effects=True, vmem_limit_bytes=62 * 1024 * 1024),
        name="reduce_blocks",
    )(places, starts, counts, hidden, grad_out)


def on_device(hidden, grad_out, block_row, block_col, owner_of, master, moment1, moment2):
    share = master.shape[1]
    places, starts, counts = sorted_places(owner_of, block_row, block_col, lax.axis_index("owner"))
    shares, total = reduce_blocks(places, starts, counts, hidden, grad_out, share)
    clip = 1.0 / jnp.maximum(jnp.sqrt(total[0, 0]), 1.0)
    scaled = clip * shares[None]
    first = 0.9 * moment1 + 0.1 * scaled
    second = 0.95 * moment2 + 0.05 * scaled * scaled
    direction = first / (1.0 - 0.9**10) / (jnp.sqrt(second / (1.0 - 0.95**10)) + 1e-08)
    return master - 0.25 * (direction + 0.1 * master)


def solution(mesh):
    placed = (
        P("dp", None),
        P("dp", None),
        P(),
        P(),
        P(),
        P("owner", "dp", None, None),
        P("owner", "dp", None, None),
        P("owner", "dp", None, None),
    )
    return jax.shard_map(
        on_device,
        mesh=mesh,
        in_specs=placed,
        out_specs=P("owner", "dp", None, None),
        check_vma=False,
    )
```

```python
import functools

import jax
import jax.numpy as jnp
from jax import lax
from jax.experimental import pallas as pl
from jax.experimental.pallas import tpu as pltpu
from jax.sharding import PartitionSpec as P

BLOCK = 128
N_OWNER = 8
MESH = pl.DeviceIdType.MESH
CHUNKS = 3
CHIPS = 16
PAIR, XA, XB0, XB1, YA, YB0, YB1 = 0, 1, 3, 5, 7, 9, 11


def sorted_places(owner_of, block_row, block_col, plane):
    owners = jnp.arange(N_OWNER, dtype=jnp.int32)
    named = (owner_of[:, 0][None, :] == owners[:, None]).astype(jnp.int32)
    running = jnp.cumsum(named, axis=1)
    counts = running[:, -1]
    starts = jnp.sum(jnp.where(owners[None, :] < owners[:, None], counts[None, :], 0), axis=1)
    spot = jnp.sum(named * (running - 1 + starts[:, None]), axis=0)
    place = jnp.arange(CHUNKS * 4 * CHIPS, dtype=jnp.int32)
    chunk, pos, chip = place // (4 * CHIPS), (place // CHIPS) % 4, place % CHIPS
    wanted = CHIPS * (24 * pos + CHUNKS * plane + chunk) + chip
    packed = block_row * 32 + block_col
    listed = jnp.sum(jnp.where(wanted[:, None] == spot[None, :], packed[None, :], 0), axis=1)
    return listed, starts, counts


def wrap(value, size):
    return lax.rem(value, size)


def kernel(items, share, place_ref, start_ref, count_ref, hidden_hbm, grad_hbm, slot_grad_ref, total_ref,
           hidden, grad, grad_t, to_pair, from_pair, chip, ring_a, ring_b, line, last_a, last_b,
           done_0, done_1, done_2, to_owner, gathered, to_slot, landed,
           sums, sum_in, load_sem, send_sem, recv_sem, move_send, move_recv, sum_send, sum_recv):
    f32, bf16 = jnp.float32, jnp.bfloat16
    d = lax.axis_index("dp")
    z = lax.axis_index("owner")
    x, y, c = lax.div(d, 8), wrap(lax.div(d, 2), 4), wrap(d, 2)

    def device(px, py, pc):
        return {"dp": (px * 4 + py) * 2 + pc}

    partner = device(x, y, 1 - c)

    def near(axis, step):
        if axis == 0:
            return device(wrap(x + step, 4), y, c)
        return device(x, wrap(y + step, 4), c)

    def up(step):
        return {"owner": wrap(z + step, N_OWNER)}

    groups = [[partner], [near(0, k) for k in (1, 2, 3)], [near(1, k) for k in (1, 2, 3)],
              [up(k) for k in range(1, N_OWNER)]]
    barrier = pltpu.get_barrier_semaphore()
    offsets = [(dx, dy) for dx in range(4) for dy in range(4) if dx or dy]
    spread = [device(wrap(x + dx, 4), wrap(y + dy, 4), c) for dx, dy in offsets]
    everyone = [partner] + spread + groups[3]
    for who in everyone:
        pl.semaphore_signal(barrier, inc=1, device_id=who, device_id_type=MESH)

    def load(src, dst, sem, k):
        columns = pl.ds(pl.multiple_of(k * BLOCK, BLOCK), BLOCK)
        pltpu.make_async_copy(src.at[:, columns], dst.at[k], sem).start()

    def load_grad(k, carry):
        load(grad_hbm, grad, load_sem.at[0], k)
        return carry

    lax.fori_loop(0, grad.shape[0], load_grad, 0, unroll=8)

    def load_hidden(k, carry):
        load(hidden_hbm, hidden, load_sem.at[1], k)
        return carry

    early = hidden.shape[0] // 2
    lax.fori_loop(0, early, load_hidden, 0, unroll=8)
    pltpu.make_async_copy(grad, grad, load_sem.at[0]).wait()

    def turn(k, carry):
        for n in range(2):
            load(hidden_hbm, hidden, load_sem.at[1], early + 2 * k + n)
        grad_t[k] = grad[k].T
        return carry

    late = hidden.shape[0] - early
    lax.fori_loop(0, late // 2, turn, 0, unroll=4)

    def turn_only(k, carry):
        grad_t[k] = grad[k].T
        return carry

    lax.fori_loop(late // 2, grad.shape[0], turn_only, 0, unroll=4)
    pltpu.make_async_copy(hidden, hidden, load_sem.at[1]).wait()

    started = []

    def send(src, dst, item, kind, who):
        copy = pltpu.make_async_remote_copy(
            src_ref=src, dst_ref=dst, send_sem=send_sem.at[item, kind],
            recv_sem=recv_sem.at[item, kind], device_id=who, device_id_type=MESH)
        copy.start()
        started.append(copy)
        arrivals[item, kind] = copy

    arrivals = {}

    def arrive(item, kind):
        arrivals[item, kind].wait_recv()

    def product(place):
        both_indices = place_ref[place]
        row, col = lax.shift_right_logical(both_indices, 5), both_indices & 31
        return jnp.dot(grad_t[col], hidden[row], preferred_element_type=f32)

    def slot_of(item, ra, rb, core):
        if item % 2 == 0:
            px, py = wrap(x + ra, 4), wrap(y + rb, 4)
        else:
            px, py = wrap(x + rb, 4), wrap(y + ra, 4)
        return ((item // 2) * 4 + 2 * core + item % 2) * CHIPS + px * 4 + py

    def partner_products(item):
        for j in range(CHIPS):
            to_pair[item, j] = product(slot_of(item, j // 4, j % 4, 1 - c)).astype(bf16)
        if item == 0:
            pl.semaphore_wait(barrier, len(everyone))
        send(to_pair.at[item], from_pair.at[item], item, PAIR, partner)

    def own_products(item):
        arrive(item, PAIR)

        for j in range(CHIPS):
            value = product(slot_of(item, j // 4, j % 4, c)) + from_pair[item, j].astype(f32)
            chip[item, j] = value.astype(bf16)
        axis = item % 2
        send(chip.at[item, pl.ds(8, 2)], ring_a.at[item, 0], item, XA, near(axis, 1))
        send(chip.at[item, pl.ds(10, 2)], ring_a.at[item, 1], item, XA + 1, near(axis, 3))
        send(chip.at[item, pl.ds(6, 2)], ring_b.at[item, 0, pl.ds(2, 2)], item, XB0, near(axis, 1))
        send(chip.at[item, pl.ds(12, 2)], ring_b.at[item, 1, pl.ds(0, 2)], item, XB0 + 1, near(axis, 3))

    def ring_step(item):
        axis = item % 2
        arrive(item, XA)
        chip[item, 4:6] = (chip[item, 4:6].astype(f32) + ring_a[item, 0].astype(f32)).astype(bf16)
        send(chip.at[item, pl.ds(4, 2)], ring_b.at[item, 0, pl.ds(0, 2)], item, XB1, near(axis, 1))
        arrive(item, XA + 1)
        chip[item, 14:16] = (chip[item, 14:16].astype(f32) + ring_a[item, 1].astype(f32)).astype(bf16)
        send(chip.at[item, pl.ds(14, 2)], ring_b.at[item, 1, pl.ds(2, 2)], item, XB1 + 1, near(axis, 3))

    def ring_end(item):
        axis = 1 - item % 2
        for kind in (XB0, XB0 + 1, XB1, XB1 + 1):
            arrive(item, kind)
        for rb in (2, 1, 3, 0):
            value = (chip[item, rb].astype(f32) + ring_b[item, 0, rb].astype(f32)
                     + ring_b[item, 1, rb].astype(f32))
            line[item, rb] = value.astype(bf16)
        half = BLOCK // 2
        low, high = pl.ds(0, half), pl.ds(half, half)
        send(line.at[item, 2, low], last_a.at[item, 0], item, YA, near(axis, 1))
        send(line.at[item, 2, high], last_a.at[item, 1], item, YA + 1, near(axis, 3))
        send(line.at[item, 1, high], last_b.at[item, 0, high], item, YB0, near(axis, 1))
        send(line.at[item, 3, low], last_b.at[item, 1, low], item, YB0 + 1, near(axis, 3))

    def line_step(item):
        axis = 1 - item % 2
        half = BLOCK // 2
        low, high = pl.ds(0, half), pl.ds(half, half)
        arrive(item, YA)
        line[item, 1, :half] = (line[item, 1, :half].astype(f32) + last_a[item, 0].astype(f32)).astype(bf16)
        send(line.at[item, 1, low], last_b.at[item, 0, low], item, YB1, near(axis, 1))
        arrive(item, YA + 1)
        line[item, 3, half:] = (line[item, 3, half:].astype(f32) + last_a[item, 1].astype(f32)).astype(bf16)
        send(line.at[item, 3, high], last_b.at[item, 1, high], item, YB1 + 1, near(axis, 3))

    def finish(item):
        for kind in (YB0, YB0 + 1, YB1, YB1 + 1):
            arrive(item, kind)
        value = (line[item, 0].astype(f32) + last_b[item, 0].astype(f32) + last_b[item, 1].astype(f32))
        done[item // 2][c * 2 + item % 2] = value.astype(bf16)
        return jnp.sum((value * value).reshape(-1, 8, BLOCK), axis=0)

    done = (done_0, done_1, done_2)
    me_chip = x * 4 + y
    half = BLOCK // 2
    mine = pl.ds(pl.multiple_of(c * half, half), half)
    moves = {}

    def move(src, dst, index, who):
        copy = pltpu.make_async_remote_copy(
            src_ref=src, dst_ref=dst, send_sem=move_send.at[index], recv_sem=move_recv.at[index],
            device_id=who, device_id_type=MESH)
        copy.start()
        started.append(copy)
        moves[index] = copy

    def share_done(chunk):
        move(done[chunk].at[pl.ds(2 * c, 2)], done[chunk].at[pl.ds(2 * c, 2)], chunk, partner)

    def held_for(chunk, owner):
        first = start_ref[owner] - me_chip - CHIPS * (CHUNKS * z + chunk) + 383
        pos = jnp.minimum(lax.div(jnp.maximum(first, 0), 384), 3)
        return done[chunk][pos]

    def to_owners(chunk):
        moves[chunk].wait_recv()
        base = 3 + 6 * chunk
        for j in (1, 2, 0):
            owner = wrap(z + 2 * j + 1 + c, N_OWNER)
            to_owner[chunk, j] = held_for(chunk, owner)
            move(to_owner.at[chunk, j], gathered.at[chunk * 8 + c * 3 + j], base + j, {"owner": owner})
        owner = wrap(z + 7, N_OWNER)
        to_owner[chunk, 3] = held_for(chunk, owner)
        move(to_owner.at[chunk, 3, mine], gathered.at[chunk * 8 + 6, mine], base + 3, {"owner": owner})
        gathered[chunk * 8 + 7] = held_for(chunk, z)

    def share_gathered(chunk):
        base = 3 + 6 * chunk
        for j in range(4):
            moves[base + j].wait_recv()
        trio = gathered.at[pl.ds(chunk * 8 + c * 3, 3)]
        move(trio, trio, base + 4, partner)
        rest = gathered.at[chunk * 8 + 6, mine]
        move(rest, rest, base + 5, partner)

    start, count = start_ref[z], count_ref[z]

    def block_for(to_chip):
        first = start + share * (2 * to_chip + c)
        spot = first + ((me_chip - first) & (CHIPS - 1))
        q = jnp.minimum(lax.div(spot, CHIPS), 95)
        chunk = wrap(q, CHUNKS)
        away = (z - lax.div(q, CHUNKS)) & (N_OWNER - 1)
        index = 3 * ((away + 1) & 1) + lax.shift_right_logical(away + 7, 1) - 4
        index = jnp.where(away == 0, 7, jnp.where(away == 7, 6, index))
        return gathered[chunk * 8 + index]

    def to_slots():
        for chunk in range(CHUNKS):
            moves[3 + 6 * chunk + 4].wait_recv()
            moves[3 + 6 * chunk + 5].wait_recv()
        base = 3 + 6 * CHUNKS
        for k, (dx, dy) in enumerate(offsets):
            to_slot[k] = block_for(wrap(x + dx, 4) * 4 + wrap(y + dy, 4))
            move(to_slot.at[k], landed.at[me_chip], base + k, spread[k])
        landed[me_chip] = block_for(me_chip)

    def store_slots():
        for k in range(len(offsets)):
            moves[3 + 6 * CHUNKS + k].wait_recv()
        for i in range(share):
            slot = d * share + i
            value = landed[(start + slot) & (CHIPS - 1)].astype(f32)
            slot_grad_ref[i] = (value * (slot < count).astype(f32)).T

    def add_start(n, value):
        first = sum(len(group) for group in groups[:n])
        sums[n] = value
        copies = []
        for k, who in enumerate(groups[n]):
            copy = pltpu.make_async_remote_copy(
                src_ref=sums.at[n], dst_ref=sum_in.at[first + k], send_sem=sum_send.at[first + k],
                recv_sem=sum_recv.at[first + k], device_id=who, device_id_type=MESH)
            copy.start()
            started.append(copy)
            copies.append((first + k, copy))
        return copies

    def add_end(value, copies):
        for k, copy in copies:
            copy.wait_recv()
            value = value + sum_in[k]
        return value

    part = jnp.zeros((8, BLOCK), f32)

    def pair(stage, chunk):
        return [stage(2 * chunk), stage(2 * chunk + 1)]

    def close(chunk, value):
        for piece in pair(finish, chunk):
            value = value + piece
        share_done(chunk)
        return value

    pair(partner_products, 0)
    pair(partner_products, 1)
    pair(own_products, 0)
    pair(partner_products, 2)
    pair(own_products, 1)
    pair(ring_step, 0)
    pair(own_products, 2)
    pair(ring_step, 1)
    pair(ring_end, 0)
    pair(ring_step, 2)
    pair(line_step, 0)
    pair(ring_end, 1)
    part = close(0, part)
    pair(ring_end, 2)
    pair(line_step, 1)
    to_owners(0)
    part = close(1, part)
    pair(line_step, 2)
    to_owners(1)
    part = close(2, part)
    copies = add_start(0, part)
    to_owners(2)
    share_gathered(0)
    part = add_end(part, copies)
    copies = add_start(1, part)
    share_gathered(1)
    share_gathered(2)
    part = add_end(part, copies)
    copies = add_start(2, part)
    to_slots()
    part = add_end(part, copies)
    copies = add_start(3, part)
    store_slots()
    part = add_end(part, copies)
    total_ref[0, 0] = jnp.sum(part)
    for copy in started:
        copy.wait_send()


def reduce_blocks(places, starts, counts, hidden, grad_out, share):
    tokens, features = hidden.shape[0], grad_out.shape[1]
    bf16, f32 = jnp.bfloat16, jnp.float32
    items = 2 * CHUNKS
    peers = 1 + 3 + 3 + N_OWNER - 1
    block = (BLOCK, BLOCK)
    smem = pl.BlockSpec(memory_space=pltpu.SMEM)
    vmem = pl.BlockSpec(memory_space=pltpu.VMEM)
    hbm = pl.BlockSpec(memory_space=pl.ANY)
    return pl.pallas_call(
        functools.partial(kernel, items, share),
        out_shape=(jax.ShapeDtypeStruct((share, *block), f32), jax.ShapeDtypeStruct((1, 1), f32)),
        in_specs=[smem, smem, smem, hbm, hbm],
        out_specs=(vmem, smem),
        scratch_shapes=[
            pltpu.VMEM((hidden.shape[1] // BLOCK, tokens, BLOCK), bf16),
            pltpu.VMEM((features // BLOCK, tokens, BLOCK), bf16),
            pltpu.VMEM((features // BLOCK, BLOCK, tokens), bf16),
            pltpu.VMEM((items, 16, *block), bf16),
            pltpu.VMEM((items, 16, *block), bf16),
            pltpu.VMEM((items, 16, *block), bf16),
            pltpu.VMEM((items, 2, 2, *block), bf16),
            pltpu.VMEM((items, 2, 4, *block), bf16),
            pltpu.VMEM((items, 4, *block), bf16),
            pltpu.VMEM((items, 2, BLOCK // 2, BLOCK), bf16),
            pltpu.VMEM((items, 2, *block), bf16),
            pltpu.VMEM((4, *block), bf16),
            pltpu.VMEM((4, *block), bf16),
            pltpu.VMEM((4, *block), bf16),
            pltpu.VMEM((CHUNKS, 4, *block), bf16),
            pltpu.VMEM((CHUNKS * N_OWNER, *block), bf16),
            pltpu.VMEM((CHIPS - 1, *block), bf16),
            pltpu.VMEM((CHIPS, *block), bf16),
            pltpu.VMEM((4, 8, BLOCK), f32),
            pltpu.VMEM((peers, 8, BLOCK), f32),
            pltpu.SemaphoreType.DMA((2,)),
            pltpu.SemaphoreType.DMA((items, 13)),
            pltpu.SemaphoreType.DMA((items, 13)),
            pltpu.SemaphoreType.DMA((7 * CHUNKS + CHIPS - 1,)),
            pltpu.SemaphoreType.DMA((7 * CHUNKS + CHIPS - 1,)),
            pltpu.SemaphoreType.DMA((peers,)),
            pltpu.SemaphoreType.DMA((peers,)),
        ],
        compiler_params=pltpu.CompilerParams(
            collective_id=0, has_side_effects=True, vmem_limit_bytes=62 * 1024 * 1024),
        name="reduce_blocks",
    )(places, starts, counts, hidden, grad_out)


def on_device(hidden, grad_out, block_row, block_col, owner_of, master, moment1, moment2):
    share = master.shape[1]
    places, starts, counts = sorted_places(owner_of, block_row, block_col, lax.axis_index("owner"))
    shares, total = reduce_blocks(places, starts, counts, hidden, grad_out, share)
    clip = 1.0 / jnp.maximum(jnp.sqrt(total[0, 0]), 1.0)
    scaled = clip * shares[None]
    first = 0.9 * moment1 + 0.1 * scaled
    second = 0.95 * moment2 + 0.05 * scaled * scaled
    direction = first / (1.0 - 0.9**10) / (jnp.sqrt(second / (1.0 - 0.95**10)) + 1e-08)
    return master - 0.25 * (direction + 0.1 * master)


def solution(mesh):
    placed = (
        P("dp", None),
        P("dp", None),
        P(),
        P(),
        P(),
        P("owner", "dp", None, None),
        P("owner", "dp", None, None),
        P("owner", "dp", None, None),
    )
    return jax.shard_map(
        on_device,
        mesh=mesh,
        in_specs=placed,
        out_specs=P("owner", "dp", None, None),
        check_vma=False,
    )
```

```python
import functools

import jax
import jax.numpy as jnp
from jax import lax
from jax.experimental import pallas as pl
from jax.experimental.pallas import tpu as pltpu
from jax.sharding import PartitionSpec as P

BLOCK = 128
N_OWNER = 8
MESH = pl.DeviceIdType.MESH
CHUNKS = 3
CHIPS = 16
PAIR, XA, XB0, XB1, YA, YB0, YB1 = 0, 1, 3, 5, 7, 9, 11


def wrap(value, size):
    return lax.rem(value, size)


def kernel(items, share, listed, row_ref, col_ref, owner_ref, hidden_hbm, grad_hbm, slot_grad_ref, total_ref,
           spots_v, starts_v, spots, starts, hidden, grad, grad_t, to_pair, from_pair, chip, ring_a, ring_b, line, last_a, last_b,
           done_0, done_1, done_2, to_owner, gathered, to_slot, landed,
           sums, sum_in, load_sem, send_sem, recv_sem, move_send, move_recv, sum_send, sum_recv):
    f32, bf16 = jnp.float32, jnp.bfloat16
    d = lax.axis_index("dp")
    z = lax.axis_index("owner")
    x, y, c = lax.div(d, 8), wrap(lax.div(d, 2), 4), wrap(d, 2)

    def device(px, py, pc):
        return {"dp": (px * 4 + py) * 2 + pc}

    partner = device(x, y, 1 - c)

    def near(axis, step):
        if axis == 0:
            return device(wrap(x + step, 4), y, c)
        return device(x, wrap(y + step, 4), c)

    def up(step):
        return {"owner": wrap(z + step, N_OWNER)}

    groups = [[partner], [near(0, k) for k in (1, 2, 3)], [near(1, k) for k in (1, 2, 3)],
              [up(k) for k in range(1, N_OWNER)]]
    barrier = pltpu.get_barrier_semaphore()
    offsets = [(dx, dy) for dx in range(4) for dy in range(4) if dx or dy]
    spread = [device(wrap(x + dx, 4), wrap(y + dy, 4), c) for dx, dy in offsets]
    everyone = [partner] + spread + groups[3]
    for who in everyone:
        pl.semaphore_signal(barrier, inc=1, device_id=who, device_id_type=MESH)

    def load(src, dst, sem, k):
        columns = pl.ds(pl.multiple_of(k * BLOCK, BLOCK), BLOCK)
        pltpu.make_async_copy(src.at[:, columns], dst.at[k], sem).start()

    def load_grad(k, carry):
        load(grad_hbm, grad, load_sem.at[0], k)
        return carry

    lax.fori_loop(0, grad.shape[0], load_grad, 0, unroll=8)

    def load_hidden(k, carry):
        load(hidden_hbm, hidden, load_sem.at[1], k)
        return carry

    def make_places():
        square = (BLOCK, BLOCK)
        lines = listed // BLOCK
        up_to = lax.broadcasted_iota(jnp.int32, square, 0) <= lax.broadcasted_iota(jnp.int32, square, 1)
        below = lax.broadcasted_iota(jnp.int32, square, 1) < lax.broadcasted_iota(jnp.int32, square, 0)
        owners = owner_ref[...]
        named = jnp.concatenate([(owners == o).astype(f32) for o in range(N_OWNER)], axis=0)
        named_16 = named.astype(bf16)
        along = jnp.dot(named_16, up_to.astype(f32).astype(bf16), preferred_element_type=f32)
        line_sums = jnp.dot(named_16, jnp.ones(square, bf16), preferred_element_type=f32)
        before = jnp.dot(below.astype(f32).astype(bf16), line_sums.astype(bf16), preferred_element_type=f32)
        spot = jnp.sum((named * (before + along - 1.0)).reshape(N_OWNER, -1, BLOCK), axis=0)
        starts_v[...] = before.reshape(N_OWNER, -1, BLOCK)[:, 0].astype(jnp.int32)
        spot_t = jnp.pad(spot, ((0, BLOCK - spot.shape[0]), (0, 0))).T
        wide = (BLOCK, 2 * BLOCK)
        place = lax.broadcasted_iota(jnp.int32, wide, 1)
        chip_of, pos, chunk = place & (CHIPS - 1), lax.shift_right_logical(place, 4) & 3, lax.shift_right_logical(place, 6)
        wanted = (CHIPS * (24 * pos + CHUNKS * z + chunk) + chip_of).astype(f32)
        which = lax.broadcasted_iota(jnp.int32, (8, BLOCK), 0)
        found = jnp.zeros((8, 2 * BLOCK), f32)
        for r in range(lines):
            hit = jnp.where(spot_t[:, r:r + 1] == wanted, 1.0, 0.0).astype(bf16)
            value = jnp.where(which == 0, row_ref[r:r + 1, :], col_ref[r:r + 1, :]).astype(f32).astype(bf16)
            found = found + jnp.dot(value, hit, preferred_element_type=f32)
        spots_v[...] = found.astype(jnp.int32)
        copies = [pltpu.make_async_copy(spots_v, spots, load_sem.at[2]),
                  pltpu.make_async_copy(starts_v, starts, load_sem.at[3])]
        for copy in copies:
            copy.start()
        for copy in copies:
            copy.wait()

    early = hidden.shape[0] // 2
    lax.fori_loop(0, early, load_hidden, 0, unroll=8)
    make_places()
    pltpu.make_async_copy(grad, grad, load_sem.at[0]).wait()

    def turn(k, carry):
        for n in range(2):
            load(hidden_hbm, hidden, load_sem.at[1], early + 2 * k + n)
        grad_t[k] = grad[k].T
        return carry

    late = hidden.shape[0] - early
    lax.fori_loop(0, late // 2, turn, 0, unroll=4)

    def turn_only(k, carry):
        grad_t[k] = grad[k].T
        return carry

    lax.fori_loop(late // 2, grad.shape[0], turn_only, 0, unroll=4)
    pltpu.make_async_copy(hidden, hidden, load_sem.at[1]).wait()

    started = []

    def send(src, dst, item, kind, who):
        copy = pltpu.make_async_remote_copy(
            src_ref=src, dst_ref=dst, send_sem=send_sem.at[item, kind],
            recv_sem=recv_sem.at[item, kind], device_id=who, device_id_type=MESH)
        copy.start()
        started.append(copy)
        arrivals[item, kind] = copy

    arrivals = {}

    def arrive(item, kind):
        arrivals[item, kind].wait_recv()

    def product(place):
        row = jnp.clip(spots[0, place], 0, hidden.shape[0] - 1)
        col = jnp.clip(spots[1, place], 0, grad_t.shape[0] - 1)
        return jnp.dot(grad_t[col], hidden[row], preferred_element_type=f32)

    def slot_of(item, ra, rb, core):
        if item % 2 == 0:
            px, py = wrap(x + ra, 4), wrap(y + rb, 4)
        else:
            px, py = wrap(x + rb, 4), wrap(y + ra, 4)
        return ((item // 2) * 4 + 2 * core + item % 2) * CHIPS + px * 4 + py

    def partner_products(item):
        for j in range(CHIPS):
            to_pair[item, j] = product(slot_of(item, j // 4, j % 4, 1 - c)).astype(bf16)
        if item == 0:
            pl.semaphore_wait(barrier, len(everyone))
        send(to_pair.at[item], from_pair.at[item], item, PAIR, partner)

    def own_products(item):
        arrive(item, PAIR)

        for j in range(CHIPS):
            value = product(slot_of(item, j // 4, j % 4, c)) + from_pair[item, j].astype(f32)
            chip[item, j] = value.astype(bf16)
        axis = item % 2
        send(chip.at[item, pl.ds(8, 2)], ring_a.at[item, 0], item, XA, near(axis, 1))
        send(chip.at[item, pl.ds(10, 2)], ring_a.at[item, 1], item, XA + 1, near(axis, 3))
        send(chip.at[item, pl.ds(6, 2)], ring_b.at[item, 0, pl.ds(2, 2)], item, XB0, near(axis, 1))
        send(chip.at[item, pl.ds(12, 2)], ring_b.at[item, 1, pl.ds(0, 2)], item, XB0 + 1, near(axis, 3))

    def ring_step(item):
        axis = item % 2
        arrive(item, XA)
        chip[item, 4:6] = (chip[item, 4:6].astype(f32) + ring_a[item, 0].astype(f32)).astype(bf16)
        send(chip.at[item, pl.ds(4, 2)], ring_b.at[item, 0, pl.ds(0, 2)], item, XB1, near(axis, 1))
        arrive(item, XA + 1)
        chip[item, 14:16] = (chip[item, 14:16].astype(f32) + ring_a[item, 1].astype(f32)).astype(bf16)
        send(chip.at[item, pl.ds(14, 2)], ring_b.at[item, 1, pl.ds(2, 2)], item, XB1 + 1, near(axis, 3))

    def ring_end(item):
        axis = 1 - item % 2
        for kind in (XB0, XB0 + 1, XB1, XB1 + 1):
            arrive(item, kind)
        for rb in (2, 1, 3, 0):
            value = (chip[item, rb].astype(f32) + ring_b[item, 0, rb].astype(f32)
                     + ring_b[item, 1, rb].astype(f32))
            line[item, rb] = value.astype(bf16)
        half = BLOCK // 2
        low, high = pl.ds(0, half), pl.ds(half, half)
        send(line.at[item, 2, low], last_a.at[item, 0], item, YA, near(axis, 1))
        send(line.at[item, 2, high], last_a.at[item, 1], item, YA + 1, near(axis, 3))
        send(line.at[item, 1, high], last_b.at[item, 0, high], item, YB0, near(axis, 1))
        send(line.at[item, 3, low], last_b.at[item, 1, low], item, YB0 + 1, near(axis, 3))

    def line_step(item):
        axis = 1 - item % 2
        half = BLOCK // 2
        low, high = pl.ds(0, half), pl.ds(half, half)
        arrive(item, YA)
        line[item, 1, :half] = (line[item, 1, :half].astype(f32) + last_a[item, 0].astype(f32)).astype(bf16)
        send(line.at[item, 1, low], last_b.at[item, 0, low], item, YB1, near(axis, 1))
        arrive(item, YA + 1)
        line[item, 3, half:] = (line[item, 3, half:].astype(f32) + last_a[item, 1].astype(f32)).astype(bf16)
        send(line.at[item, 3, high], last_b.at[item, 1, high], item, YB1 + 1, near(axis, 3))

    def finish(item):
        for kind in (YB0, YB0 + 1, YB1, YB1 + 1):
            arrive(item, kind)
        value = (line[item, 0].astype(f32) + last_b[item, 0].astype(f32) + last_b[item, 1].astype(f32))
        done[item // 2][c * 2 + item % 2] = value.astype(bf16)
        return jnp.sum((value * value).reshape(-1, 8, BLOCK), axis=0)

    done = (done_0, done_1, done_2)
    me_chip = x * 4 + y
    half = BLOCK // 2
    mine = pl.ds(pl.multiple_of(c * half, half), half)
    moves = {}

    def move(src, dst, index, who):
        copy = pltpu.make_async_remote_copy(
            src_ref=src, dst_ref=dst, send_sem=move_send.at[index], recv_sem=move_recv.at[index],
            device_id=who, device_id_type=MESH)
        copy.start()
        started.append(copy)
        moves[index] = copy

    def share_done(chunk):
        move(done[chunk].at[pl.ds(2 * c, 2)], done[chunk].at[pl.ds(2 * c, 2)], chunk, partner)

    def held_for(chunk, owner):
        first = jnp.clip(starts[owner, 0], 0, listed) - me_chip - CHIPS * (CHUNKS * z + chunk) + 383
        pos = jnp.minimum(lax.div(jnp.maximum(first, 0), 384), 3)
        return done[chunk][pos]

    def to_owners(chunk):
        moves[chunk].wait_recv()
        base = 3 + 6 * chunk
        for j in (1, 2, 0):
            owner = wrap(z + 2 * j + 1 + c, N_OWNER)
            to_owner[chunk, j] = held_for(chunk, owner)
            move(to_owner.at[chunk, j], gathered.at[chunk * 8 + c * 3 + j], base + j, {"owner": owner})
        owner = wrap(z + 7, N_OWNER)
        to_owner[chunk, 3] = held_for(chunk, owner)
        move(to_owner.at[chunk, 3, mine], gathered.at[chunk * 8 + 6, mine], base + 3, {"owner": owner})
        gathered[chunk * 8 + 7] = held_for(chunk, z)

    def share_gathered(chunk):
        base = 3 + 6 * chunk
        for j in range(4):
            moves[base + j].wait_recv()
        trio = gathered.at[pl.ds(chunk * 8 + c * 3, 3)]
        move(trio, trio, base + 4, partner)
        rest = gathered.at[chunk * 8 + 6, mine]
        move(rest, rest, base + 5, partner)

    start = jnp.clip(starts[z, 0], 0, listed)
    count = jnp.where(z == N_OWNER - 1, listed, starts[jnp.minimum(z + 1, N_OWNER - 1), 0]) - start

    def block_for(to_chip):
        first = start + share * (2 * to_chip + c)
        spot = first + ((me_chip - first) & (CHIPS - 1))
        q = jnp.minimum(lax.div(spot, CHIPS), 95)
        chunk = wrap(q, CHUNKS)
        away = (z - lax.div(q, CHUNKS)) & (N_OWNER - 1)
        index = 3 * ((away + 1) & 1) + lax.shift_right_logical(away + 7, 1) - 4
        index = jnp.where(away == 0, 7, jnp.where(away == 7, 6, index))
        return gathered[chunk * 8 + index]

    def to_slots():
        for chunk in range(CHUNKS):
            moves[3 + 6 * chunk + 4].wait_recv()
            moves[3 + 6 * chunk + 5].wait_recv()
        base = 3 + 6 * CHUNKS
        for k, (dx, dy) in enumerate(offsets):
            to_slot[k] = block_for(wrap(x + dx, 4) * 4 + wrap(y + dy, 4))
            move(to_slot.at[k], landed.at[me_chip], base + k, spread[k])
        landed[me_chip] = block_for(me_chip)

    def store_slots():
        for k in range(len(offsets)):
            moves[3 + 6 * CHUNKS + k].wait_recv()
        for i in range(share):
            slot = d * share + i
            value = landed[(start + slot) & (CHIPS - 1)].astype(f32)
            slot_grad_ref[i] = (value * (slot < count).astype(f32)).T

    def add_start(n, value):
        first = sum(len(group) for group in groups[:n])
        sums[n] = value
        copies = []
        for k, who in enumerate(groups[n]):
            copy = pltpu.make_async_remote_copy(
                src_ref=sums.at[n], dst_ref=sum_in.at[first + k], send_sem=sum_send.at[first + k],
                recv_sem=sum_recv.at[first + k], device_id=who, device_id_type=MESH)
            copy.start()
            started.append(copy)
            copies.append((first + k, copy))
        return copies

    def add_end(value, copies):
        for k, copy in copies:
            copy.wait_recv()
            value = value + sum_in[k]
        return value

    part = jnp.zeros((8, BLOCK), f32)

    def pair(stage, chunk):
        return [stage(2 * chunk), stage(2 * chunk + 1)]

    def close(chunk, value):
        for piece in pair(finish, chunk):
            value = value + piece
        share_done(chunk)
        return value

    pair(partner_products, 0)
    pair(partner_products, 1)
    pair(own_products, 0)
    pair(partner_products, 2)
    pair(own_products, 1)
    pair(ring_step, 0)
    pair(own_products, 2)
    pair(ring_step, 1)
    pair(ring_end, 0)
    pair(ring_step, 2)
    pair(line_step, 0)
    pair(ring_end, 1)
    part = close(0, part)
    pair(ring_end, 2)
    pair(line_step, 1)
    to_owners(0)
    part = close(1, part)
    pair(line_step, 2)
    to_owners(1)
    part = close(2, part)
    copies = add_start(0, part)
    to_owners(2)
    share_gathered(0)
    part = add_end(part, copies)
    copies = add_start(1, part)
    share_gathered(1)
    share_gathered(2)
    part = add_end(part, copies)
    copies = add_start(2, part)
    to_slots()
    part = add_end(part, copies)
    copies = add_start(3, part)
    store_slots()
    part = add_end(part, copies)
    total_ref[0, 0] = jnp.sum(part)
    for copy in started:
        copy.wait_send()


def reduce_blocks(block_row, block_col, owner_of, hidden, grad_out, share):
    listed = block_row.shape[0]
    tokens, features = hidden.shape[0], grad_out.shape[1]
    bf16, f32 = jnp.bfloat16, jnp.float32
    items = 2 * CHUNKS
    peers = 1 + 3 + 3 + N_OWNER - 1
    block = (BLOCK, BLOCK)
    owners = jnp.pad(owner_of.reshape(-1, BLOCK), ((0, 16 - listed // BLOCK), (0, 0)), constant_values=-1)
    smem = pl.BlockSpec(memory_space=pltpu.SMEM)
    vmem = pl.BlockSpec(memory_space=pltpu.VMEM)
    hbm = pl.BlockSpec(memory_space=pl.ANY)
    return pl.pallas_call(
        functools.partial(kernel, items, share, listed),
        out_shape=(jax.ShapeDtypeStruct((share, *block), f32), jax.ShapeDtypeStruct((1, 1), f32)),
        in_specs=[vmem, vmem, vmem, hbm, hbm],
        out_specs=(vmem, smem),
        scratch_shapes=[
            pltpu.VMEM((8, 2 * BLOCK), jnp.int32),
            pltpu.VMEM((N_OWNER, BLOCK), jnp.int32),
            pltpu.SMEM((8, 2 * BLOCK), jnp.int32),
            pltpu.SMEM((N_OWNER, BLOCK), jnp.int32),
            pltpu.VMEM((hidden.shape[1] // BLOCK, tokens, BLOCK), bf16),
            pltpu.VMEM((features // BLOCK, tokens, BLOCK), bf16),
            pltpu.VMEM((features // BLOCK, BLOCK, tokens), bf16),
            pltpu.VMEM((items, 16, *block), bf16),
            pltpu.VMEM((items, 16, *block), bf16),
            pltpu.VMEM((items, 16, *block), bf16),
            pltpu.VMEM((items, 2, 2, *block), bf16),
            pltpu.VMEM((items, 2, 4, *block), bf16),
            pltpu.VMEM((items, 4, *block), bf16),
            pltpu.VMEM((items, 2, BLOCK // 2, BLOCK), bf16),
            pltpu.VMEM((items, 2, *block), bf16),
            pltpu.VMEM((4, *block), bf16),
            pltpu.VMEM((4, *block), bf16),
            pltpu.VMEM((4, *block), bf16),
            pltpu.VMEM((CHUNKS, 4, *block), bf16),
            pltpu.VMEM((CHUNKS * N_OWNER, *block), bf16),
            pltpu.VMEM((CHIPS - 1, *block), bf16),
            pltpu.VMEM((CHIPS, *block), bf16),
            pltpu.VMEM((4, 8, BLOCK), f32),
            pltpu.VMEM((peers, 8, BLOCK), f32),
            pltpu.SemaphoreType.DMA((4,)),
            pltpu.SemaphoreType.DMA((items, 13)),
            pltpu.SemaphoreType.DMA((items, 13)),
            pltpu.SemaphoreType.DMA((7 * CHUNKS + CHIPS - 1,)),
            pltpu.SemaphoreType.DMA((7 * CHUNKS + CHIPS - 1,)),
            pltpu.SemaphoreType.DMA((peers,)),
            pltpu.SemaphoreType.DMA((peers,)),
        ],
        compiler_params=pltpu.CompilerParams(
            collective_id=0, has_side_effects=True, vmem_limit_bytes=62 * 1024 * 1024),
        name="reduce_blocks",
    )(block_row.reshape(-1, BLOCK), block_col.reshape(-1, BLOCK), owners, hidden, grad_out)


def on_device(hidden, grad_out, block_row, block_col, owner_of, master, moment1, moment2):
    share = master.shape[1]
    shares, total = reduce_blocks(block_row, block_col, owner_of, hidden, grad_out, share)
    clip = 1.0 / jnp.maximum(jnp.sqrt(total[0, 0]), 1.0)
    scaled = clip * shares[None]
    first = 0.9 * moment1 + 0.1 * scaled
    second = 0.95 * moment2 + 0.05 * scaled * scaled
    direction = first / (1.0 - 0.9**10) / (jnp.sqrt(second / (1.0 - 0.95**10)) + 1e-08)
    return master - 0.25 * (direction + 0.1 * master)


def solution(mesh):
    placed = (
        P("dp", None),
        P("dp", None),
        P(),
        P(),
        P(),
        P("owner", "dp", None, None),
        P("owner", "dp", None, None),
        P("owner", "dp", None, None),
    )
    return jax.shard_map(
        on_device,
        mesh=mesh,
        in_specs=placed,
        out_specs=P("owner", "dp", None, None),
        check_vma=False,
    )
```

```python
import functools

import jax
import jax.numpy as jnp
from jax import lax
from jax.experimental import pallas as pl
from jax.experimental.pallas import tpu as pltpu
from jax.sharding import PartitionSpec as P

BLOCK = 128
N_OWNER = 8
MESH = pl.DeviceIdType.MESH
CHUNKS = 3
ORDER = (
    "P2P3P5P4O2A2O3A3B2P0B3O4A4O5A5P1R2R3B5O0A0B4R4R5O1E2E3A1B1R0",
    "E5E4L3B0L2R1L5L4F3F2s1E0E1F5F4s2z1L0L1z2F0F1s0a0z0a0g2g1a0g0",
)
CHIPS = 16
PAIR, XA, XB, YA, YB = range(5)
DONE, OWNER, GATHER, SLOT = 0, 3, 6, 9


def wrap(value, size):
    return lax.rem(value, size)


def kernel(items, share, listed, row_hbm, col_hbm, owner_hbm, hidden_hbm, grad_hbm,
           master_hbm, moment1_hbm, moment2_hbm, updated_ref, master, moment1, moment2,
           row_ref, col_ref, owner_ref, size_ref, spots_v, starts_v, spots, starts, hidden, grad, grad_t, to_pair, from_pair, chip, ring_a, ring_b, line, last_a, last_b,
           done_0, done_1, done_2, to_owner, gathered, to_slot, landed,
           sums, sum_in, load_sem, send_sem, recv_sem, move_send, move_recv, sum_send, sum_recv):
    f32, bf16 = jnp.float32, jnp.bfloat16
    d = lax.axis_index("dp")
    z = lax.axis_index("owner")
    x, y, c = lax.div(d, 8), wrap(lax.div(d, 2), 4), wrap(d, 2)

    def device(px, py, pc):
        return {"dp": (px * 4 + py) * 2 + pc}

    partner = device(x, y, 1 - c)

    def near(axis, step):
        if axis == 0:
            return device(wrap(x + step, 4), y, c)
        return device(x, wrap(y + step, 4), c)

    lists = [pltpu.make_async_copy(src, dst, load_sem.at[7 + n]) for n, (src, dst) in enumerate(
        ((owner_hbm, owner_ref), (row_hbm, row_ref), (col_hbm, col_ref)))]
    for copy in lists:
        copy.start()

    barrier = pltpu.get_barrier_semaphore()
    offsets = [(dx, dy) for dx in range(4) for dy in range(4) if dx or dy]
    spread = [device(wrap(x + dx, 4), wrap(y + dy, 4), c) for dx, dy in offsets]
    groups = [[partner], spread, [{"owner": wrap(z + k, N_OWNER)} for k in range(1, N_OWNER)]]
    everyone = sum(groups, [])
    for who in everyone:
        pl.semaphore_signal(barrier, inc=1, device_id=who, device_id_type=MESH)

    def load(src, dst, sem, k):
        columns = pl.ds(pl.multiple_of(k * BLOCK, BLOCK), BLOCK)
        pltpu.make_async_copy(src.at[:, columns], dst.at[k], sem).start()

    def load_grad(k, carry):
        load(grad_hbm, grad, load_sem.at[0], k)
        return carry

    lax.fori_loop(0, grad.shape[0], load_grad, 0, unroll=8)

    def load_hidden(k, carry):
        load(hidden_hbm, hidden, load_sem.at[1], k)
        return carry

    def make_places():
        square = (BLOCK, BLOCK)
        lines = listed // BLOCK
        up_to = lax.broadcasted_iota(jnp.int32, square, 0) <= lax.broadcasted_iota(jnp.int32, square, 1)
        below = lax.broadcasted_iota(jnp.int32, square, 1) < lax.broadcasted_iota(jnp.int32, square, 0)
        for copy in lists:
            copy.wait()
        owners = jnp.concatenate(
            [owner_ref[:, r * BLOCK:(r + 1) * BLOCK] for r in range(lines)]
            + [jnp.full((16 - lines, BLOCK), -1, jnp.int32)], axis=0)
        named = jnp.concatenate([(owners == o).astype(f32) for o in range(N_OWNER)], axis=0)
        named_16 = named.astype(bf16)
        along = jnp.dot(named_16, up_to.astype(f32).astype(bf16), preferred_element_type=f32)
        line_sums = jnp.dot(named_16, jnp.ones(square, bf16), preferred_element_type=f32)
        before = jnp.dot(below.astype(f32).astype(bf16), line_sums.astype(bf16), preferred_element_type=f32)
        spot = jnp.sum((named * (before + along - 1.0)).reshape(N_OWNER, -1, BLOCK), axis=0)
        starts_v[...] = before.reshape(N_OWNER, -1, BLOCK)[:, 0].astype(jnp.int32)
        spot_t = jnp.pad(spot, ((0, BLOCK - spot.shape[0]), (0, 0))).T
        wide = (BLOCK, 2 * BLOCK)
        place = lax.broadcasted_iota(jnp.int32, wide, 1)
        chip_of, pos, chunk = place & (CHIPS - 1), lax.shift_right_logical(place, 4) & 3, lax.shift_right_logical(place, 6)
        wanted = (CHIPS * (24 * pos + CHUNKS * z + chunk) + chip_of).astype(f32)
        which = lax.broadcasted_iota(jnp.int32, (8, BLOCK), 0)
        found = jnp.zeros((8, 2 * BLOCK), f32)
        for r in range(lines):
            hit = jnp.where(spot_t[:, r:r + 1] == wanted, 1.0, 0.0).astype(bf16)
            value = jnp.where(which == 0, row_ref[r:r + 1, :], col_ref[r:r + 1, :]).astype(f32).astype(bf16)
            found = found + jnp.dot(value, hit, preferred_element_type=f32)
        spots_v[...] = found.astype(jnp.int32)
        copies = [pltpu.make_async_copy(spots_v, spots, load_sem.at[2]),
                  pltpu.make_async_copy(starts_v, starts, load_sem.at[3])]
        for copy in copies:
            copy.start()
        for copy in copies:
            copy.wait()

    early = hidden.shape[0] // 2
    lax.fori_loop(0, early, load_hidden, 0, unroll=8)
    make_places()
    pltpu.make_async_copy(grad, grad, load_sem.at[0]).wait()

    def turn(k, carry):
        for n in range(2):
            load(hidden_hbm, hidden, load_sem.at[1], early + 2 * k + n)
        grad_t[k] = grad[k].T
        return carry

    late = hidden.shape[0] - early
    lax.fori_loop(0, late // 2, turn, 0, unroll=4)

    def turn_only(k, carry):
        grad_t[k] = grad[k].T
        return carry

    lax.fori_loop(late // 2, grad.shape[0], turn_only, 0, unroll=4)
    pltpu.make_async_copy(hidden, hidden, load_sem.at[1]).wait()
    states = [pltpu.make_async_copy(src, dst, load_sem.at[4 + n]) for n, (src, dst) in enumerate(
        ((master_hbm, master), (moment1_hbm, moment1), (moment2_hbm, moment2)))]
    for state in states:
        state.start()

    def send(src, dst, item, kind, who):
        pltpu.make_async_remote_copy(
            src_ref=src, dst_ref=dst, send_sem=send_sem.at[kind], recv_sem=recv_sem.at[item, kind],
            device_id=who, device_id_type=MESH).start()

    def take(ref, sem):
        pltpu.make_async_copy(ref, ref, sem).wait()

    def arrive(ref, item, kind):
        take(ref.at[item], recv_sem.at[item, kind])

    def product(place):
        row = jnp.clip(spots[0, place], 0, hidden.shape[0] - 1)
        col = jnp.clip(spots[1, place], 0, grad_t.shape[0] - 1)
        return jnp.dot(grad_t[col], hidden[row], preferred_element_type=f32)

    def slot_of(item, ra, rb, core):
        if item % 2 == 0:
            px, py = wrap(x + ra, 4), wrap(y + rb, 4)
        else:
            px, py = wrap(x + rb, 4), wrap(y + ra, 4)
        return ((item // 2) * 4 + 2 * core + item % 2) * CHIPS + px * 4 + py

    def partner_products(item):
        for j in range(CHIPS):
            to_pair[item, j] = product(slot_of(item, j // 4, j % 4, 1 - c)).astype(bf16)
        if item == int(ORDER[0][1]):
            pl.semaphore_wait(barrier, len(everyone))
        send(to_pair.at[item], from_pair.at[item], item, PAIR, partner)

    def own_products(item):
        arrive(from_pair, item, PAIR)

        for j in range(CHIPS):
            value = product(slot_of(item, j // 4, j % 4, c)) + from_pair[item, j].astype(f32)
            chip[item, j] = value.astype(bf16)

    def ring_start(item):
        axis = item % 2
        send(chip.at[item, pl.ds(8, 2)], ring_a.at[item, 0], item, XA, near(axis, 1))
        send(chip.at[item, pl.ds(10, 2)], ring_a.at[item, 1], item, XA, near(axis, 3))

    def ring_own(item):
        axis = item % 2
        send(chip.at[item, pl.ds(6, 2)], ring_b.at[item, 0, pl.ds(2, 2)], item, XB, near(axis, 1))
        send(chip.at[item, pl.ds(12, 2)], ring_b.at[item, 1, pl.ds(0, 2)], item, XB, near(axis, 3))

    def ring_step(item):
        axis = item % 2
        arrive(ring_a, item, XA)
        chip[item, 4:6] = (chip[item, 4:6].astype(f32) + ring_a[item, 0].astype(f32)).astype(bf16)
        send(chip.at[item, pl.ds(4, 2)], ring_b.at[item, 0, pl.ds(0, 2)], item, XB, near(axis, 1))
        chip[item, 14:16] = (chip[item, 14:16].astype(f32) + ring_a[item, 1].astype(f32)).astype(bf16)
        send(chip.at[item, pl.ds(14, 2)], ring_b.at[item, 1, pl.ds(2, 2)], item, XB, near(axis, 3))

    def ring_end(item):
        axis = 1 - item % 2
        arrive(ring_b, item, XB)
        for rb in (2, 1, 3, 0):
            value = (chip[item, rb].astype(f32) + ring_b[item, 0, rb].astype(f32)
                     + ring_b[item, 1, rb].astype(f32))
            line[item, rb] = value.astype(bf16)
        half = BLOCK // 2
        low, high = pl.ds(0, half), pl.ds(half, half)
        send(line.at[item, 2, low], last_a.at[item, 0], item, YA, near(axis, 1))
        send(line.at[item, 2, high], last_a.at[item, 1], item, YA, near(axis, 3))
        send(line.at[item, 1, high], last_b.at[item, 0, high], item, YB, near(axis, 1))
        send(line.at[item, 3, low], last_b.at[item, 1, low], item, YB, near(axis, 3))

    def line_step(item):
        axis = 1 - item % 2
        half = BLOCK // 2
        low, high = pl.ds(0, half), pl.ds(half, half)
        arrive(last_a, item, YA)
        line[item, 1, :half] = (line[item, 1, :half].astype(f32) + last_a[item, 0].astype(f32)).astype(bf16)
        send(line.at[item, 1, low], last_b.at[item, 0, low], item, YB, near(axis, 1))
        line[item, 3, half:] = (line[item, 3, half:].astype(f32) + last_a[item, 1].astype(f32)).astype(bf16)
        send(line.at[item, 3, high], last_b.at[item, 1, high], item, YB, near(axis, 3))

    def finish(item):
        arrive(last_b, item, YB)
        value = (line[item, 0].astype(f32) + last_b[item, 0].astype(f32) + last_b[item, 1].astype(f32))
        done[item // 2][c * 2 + item % 2] = value.astype(bf16)
        return jnp.sum(value * value, axis=0, keepdims=True)

    done = (done_0, done_1, done_2)
    me_chip = x * 4 + y
    half = BLOCK // 2
    mine = pl.ds(pl.multiple_of(c * half, half), half)

    def move(src, dst, kind, index, who):
        pltpu.make_async_remote_copy(
            src_ref=src, dst_ref=dst, send_sem=move_send.at[kind + index], recv_sem=move_recv.at[kind + index],
            device_id=who, device_id_type=MESH).start()

    def share_done(chunk):
        move(done[chunk].at[pl.ds(2 * c, 2)], done[chunk].at[pl.ds(2 * c, 2)], DONE, chunk, partner)

    def held_for(chunk, owner):
        first = jnp.clip(starts[owner, 0], 0, listed) - me_chip - CHIPS * (CHUNKS * z + chunk) + 383
        pos = jnp.minimum(lax.div(jnp.maximum(first, 0), 384), 3)
        return done[chunk][pos]

    def to_owners(chunk):
        take(done[chunk].at[pl.ds(2 - 2 * c, 2)], move_recv.at[DONE + chunk])
        for j in (1, 2, 0):
            owner = wrap(z + 2 * j + 1 + c, N_OWNER)
            to_owner[chunk, j] = held_for(chunk, owner)
            move(to_owner.at[chunk, j], gathered.at[chunk * 8 + c * 3 + j], OWNER, chunk, {"owner": owner})
        owner = wrap(z + 7, N_OWNER)
        to_owner[chunk, 3] = held_for(chunk, owner)
        move(to_owner.at[chunk, 3, mine], gathered.at[chunk * 8 + 6, mine], OWNER, chunk, {"owner": owner})
        gathered[chunk * 8 + 7] = held_for(chunk, z)

    def share_gathered(chunk):
        take(size_ref, move_recv.at[OWNER + chunk])
        trio = gathered.at[pl.ds(chunk * 8 + c * 3, 3)]
        move(trio, trio, GATHER, chunk, partner)
        rest = gathered.at[chunk * 8 + 6, mine]
        move(rest, rest, GATHER, chunk, partner)

    start = jnp.clip(starts[z, 0], 0, listed)
    count = jnp.where(z == N_OWNER - 1, listed, starts[jnp.minimum(z + 1, N_OWNER - 1), 0]) - start

    def block_for(to_chip):
        first = start + share * (2 * to_chip + c)
        spot = first + ((me_chip - first) & (CHIPS - 1))
        q = jnp.minimum(lax.div(spot, CHIPS), 95)
        chunk = wrap(q, CHUNKS)
        away = (z - lax.div(q, CHUNKS)) & (N_OWNER - 1)
        index = 3 * ((away + 1) & 1) + lax.shift_right_logical(away + 7, 1) - 4
        index = jnp.where(away == 0, 7, jnp.where(away == 7, 6, index))
        return gathered[chunk * 8 + index]

    def to_slots():
        for chunk in range(CHUNKS):
            take(size_ref, move_recv.at[GATHER + chunk])
        for k in sorted(range(len(offsets)), key=lambda k: -sum(min(v, 4 - v) for v in offsets[k])):
            dx, dy = offsets[k]
            to_slot[k] = block_for(wrap(x + dx, 4) * 4 + wrap(y + dy, 4))
            move(to_slot.at[k], landed.at[me_chip], SLOT, 0, spread[k])
        landed[me_chip] = block_for(me_chip)

    def store_slots(total):
        clip = 1.0 / jnp.maximum(jnp.sqrt(jnp.full((BLOCK, BLOCK), total, f32)), 1.0)
        take(to_slot, move_recv.at[SLOT])
        for state in states:
            state.wait()
        for i in range(share):
            slot = d * share + i
            value = landed[(start + slot) & (CHIPS - 1)].astype(f32).T
            scaled = clip * (value * (slot < count).astype(f32))
            first = 0.9 * moment1[i] + 0.1 * scaled
            second = 0.95 * moment2[i] + 0.05 * scaled * scaled
            direction = first * (1.0 / (1.0 - 0.9**10)) / (jnp.sqrt(second * (1.0 / (1.0 - 0.95**10))) + 1e-08)
            updated_ref[i] = master[i] - 0.25 * (direction + 0.1 * master[i])

    def add_start(n, value):
        first = sum(len(group) for group in groups[:n])
        sums[n] = value
        for k, who in enumerate(groups[n]):
            pltpu.make_async_remote_copy(
                src_ref=sums.at[n], dst_ref=sum_in.at[first + k], send_sem=sum_send.at[0],
                recv_sem=sum_recv.at[n], device_id=who, device_id_type=MESH).start()
        return n, first

    def add_end(value, adding):
        n, first = adding
        size = len(groups[n])
        take(sum_in.at[pl.ds(first, size)], sum_recv.at[n])
        for k in range(size):
            value = value + sum_in[first + k]
        return value

    def close(item):
        parts.append(finish(item))

    parts, adding = [], []

    def add_next():
        value = adding[-1][0] if adding else functools.reduce(jnp.add, parts)
        if adding:
            value = add_end(value, adding[-1][1])
        n = len(adding)
        if n < len(groups):
            adding.append((value, add_start(n, value)))
        return value

    stages = {"P": partner_products, "O": own_products, "A": ring_start, "B": ring_own, "R": ring_step, "E": ring_end, "L": line_step,
              "F": close, "s": share_done, "z": to_owners, "g": share_gathered, "a": lambda _: add_next()}
    for name, index in zip("".join(ORDER)[::2], "".join(ORDER)[1::2]):
        stages[name](int(index))
    to_slots()
    total = jnp.sum(add_next())
    store_slots(total)
    for kind, ref in ((PAIR, to_pair), (XA, ring_a), (XB, ring_b), (YA, last_a), (YB, last_b)):
        take(ref, send_sem.at[kind])
    for chunk in range(CHUNKS):
        take(done[chunk].at[pl.ds(0, 2)], move_send.at[DONE + chunk])
        take(size_ref, move_send.at[OWNER + chunk])
        take(size_ref, move_send.at[GATHER + chunk])
    take(to_slot, move_send.at[SLOT])
    take(sum_in, sum_send.at[0])


def step(block_row, block_col, owner_of, hidden, grad_out, master, moment1, moment2):
    share = master.shape[0]
    listed = block_row.shape[0]
    tokens, features = hidden.shape[0], grad_out.shape[1]
    bf16, f32 = jnp.bfloat16, jnp.float32
    items = 2 * CHUNKS
    peers = 1 + CHIPS - 1 + N_OWNER - 1
    block = (BLOCK, BLOCK)
    vmem = pl.BlockSpec(memory_space=pltpu.VMEM)
    hbm = pl.BlockSpec(memory_space=pltpu.HBM)
    return pl.pallas_call(
        functools.partial(kernel, items, share, listed),
        out_shape=jax.ShapeDtypeStruct((share, *block), f32),
        in_specs=[hbm] * 8,
        out_specs=vmem,
        scratch_shapes=[
            pltpu.VMEM((share, *block), f32),
            pltpu.VMEM((share, *block), f32),
            pltpu.VMEM((share, *block), f32),
            pltpu.VMEM((listed // BLOCK, BLOCK), jnp.int32),
            pltpu.VMEM((listed // BLOCK, BLOCK), jnp.int32),
            pltpu.VMEM((1, listed), jnp.int32),
            pltpu.VMEM((7 * BLOCK // 2, BLOCK), bf16),
            pltpu.VMEM((8, 2 * BLOCK), jnp.int32),
            pltpu.VMEM((N_OWNER, BLOCK), jnp.int32),
            pltpu.SMEM((8, 2 * BLOCK), jnp.int32),
            pltpu.SMEM((N_OWNER, BLOCK), jnp.int32),
            pltpu.VMEM((hidden.shape[1] // BLOCK, tokens, BLOCK), bf16),
            pltpu.VMEM((features // BLOCK, tokens, BLOCK), bf16),
            pltpu.VMEM((features // BLOCK, BLOCK, tokens), bf16),
            pltpu.VMEM((items, 16, *block), bf16),
            pltpu.VMEM((items, 16, *block), bf16),
            pltpu.VMEM((items, 16, *block), bf16),
            pltpu.VMEM((items, 2, 2, *block), bf16),
            pltpu.VMEM((items, 2, 4, *block), bf16),
            pltpu.VMEM((items, 4, *block), bf16),
            pltpu.VMEM((items, 2, BLOCK // 2, BLOCK), bf16),
            pltpu.VMEM((items, 2, *block), bf16),
            pltpu.VMEM((4, *block), bf16),
            pltpu.VMEM((4, *block), bf16),
            pltpu.VMEM((4, *block), bf16),
            pltpu.VMEM((CHUNKS, 4, *block), bf16),
            pltpu.VMEM((CHUNKS * N_OWNER, *block), bf16),
            pltpu.VMEM((CHIPS - 1, *block), bf16),
            pltpu.VMEM((CHIPS, *block), bf16),
            pltpu.VMEM((3, 1, BLOCK), f32),
            pltpu.VMEM((peers, 1, BLOCK), f32),
            pltpu.SemaphoreType.DMA((10,)),
            pltpu.SemaphoreType.DMA((5,)),
            pltpu.SemaphoreType.DMA((items, 5)),
            pltpu.SemaphoreType.DMA((10,)),
            pltpu.SemaphoreType.DMA((10,)),
            pltpu.SemaphoreType.DMA((1,)),
            pltpu.SemaphoreType.DMA((3,)),
        ],
        compiler_params=pltpu.CompilerParams(
            collective_id=0, has_side_effects=True, vmem_limit_bytes=36 * 1024 * 1024),
        name="step",
    )(*[pltpu.with_memory_space_constraint(x, pltpu.HBM) for x in (
        block_row.reshape(-1, BLOCK), block_col.reshape(-1, BLOCK), owner_of.T, hidden, grad_out,
        master, moment1, moment2)])


def on_device(hidden, grad_out, block_row, block_col, owner_of, master, moment1, moment2):
    updated = step(block_row, block_col, owner_of, hidden, grad_out, master[0], moment1[0], moment2[0])
    return updated[None]


def solution(mesh):
    placed = (
        P("dp", None),
        P("dp", None),
        P(),
        P(),
        P(),
        P("owner", "dp", None, None),
        P("owner", "dp", None, None),
        P("owner", "dp", None, None),
    )
    return jax.shard_map(
        on_device,
        mesh=mesh,
        in_specs=placed,
        out_specs=P("owner", "dp", None, None),
        check_vma=False,
    )
```

```python
import functools

import jax
import jax.numpy as jnp
from jax import lax
from jax.experimental import pallas as pl
from jax.experimental.pallas import tpu as pltpu
from jax.sharding import PartitionSpec as P

BLOCK = 128
N_OWNER = 8
MESH = pl.DeviceIdType.MESH
CHUNKS = 3
ORDER = (
    "P5P4P3P2O5B5O4A4P1B4A5P0O3A3O2A2B3R4O0R5O1A0B2A1R3R2E4",
    "E5B0R1R0B1E2E3F4F5s2E1E0z2F2F3s1z1F1F0s0a0z0a0g2g1a0g0",
)
CHIPS = 16
PAIR, XA, XB, YA = range(4)
DONE, OWNER, GATHER, SLOT = 0, 3, 6, 9


def wrap(value, size):
    return lax.rem(value, size)


def kernel(items, share, listed, row_hbm, col_hbm, owner_hbm, hidden_hbm, grad_hbm,
           master_hbm, moment1_hbm, moment2_hbm, updated_ref, master, moment1, moment2,
           row_ref, col_ref, owner_ref, size_ref, spots_v, starts_v, spots, starts, hidden, grad, grad_t, to_pair, from_pair, chip, ring_a, ring_b, line, last,
           done_0, done_1, done_2, to_owner, gathered, to_slot, landed,
           sums, sum_in, load_sem, send_sem, recv_sem, move_send, move_recv, sum_send, sum_recv):
    f32, bf16 = jnp.float32, jnp.bfloat16
    d = lax.axis_index("dp")
    z = lax.axis_index("owner")
    x, y, c = lax.div(d, 8), wrap(lax.div(d, 2), 4), wrap(d, 2)

    def device(px, py, pc):
        return {"dp": (px * 4 + py) * 2 + pc}

    partner = device(x, y, 1 - c)

    def near(axis, step):
        if axis == 0:
            return device(wrap(x + step, 4), y, c)
        return device(x, wrap(y + step, 4), c)

    lists = [pltpu.make_async_copy(src, dst, load_sem.at[7 + n]) for n, (src, dst) in enumerate(
        ((owner_hbm, owner_ref), (row_hbm, row_ref), (col_hbm, col_ref)))]
    for copy in lists:
        copy.start()

    barrier = pltpu.get_barrier_semaphore()
    offsets = [(dx, dy) for dx in range(4) for dy in range(4) if dx or dy]
    spread = [device(wrap(x + dx, 4), wrap(y + dy, 4), c) for dx, dy in offsets]
    groups = [[partner], spread, [{"owner": wrap(z + k, N_OWNER)} for k in range(1, N_OWNER)]]
    everyone = sum(groups, [])
    for who in everyone:
        pl.semaphore_signal(barrier, inc=1, device_id=who, device_id_type=MESH)

    def load(src, dst, sem, k):
        columns = pl.ds(pl.multiple_of(k * BLOCK, BLOCK), BLOCK)
        pltpu.make_async_copy(src.at[:, columns], dst.at[k], sem).start()

    def load_grad(k, carry):
        load(grad_hbm, grad, load_sem.at[0], k)
        return carry

    lax.fori_loop(0, grad.shape[0], load_grad, 0, unroll=8)

    def load_hidden(k, carry):
        load(hidden_hbm, hidden, load_sem.at[1], k)
        return carry

    def make_places():
        square = (BLOCK, BLOCK)
        lines = listed // BLOCK
        up_to = lax.broadcasted_iota(jnp.int32, square, 0) <= lax.broadcasted_iota(jnp.int32, square, 1)
        below = lax.broadcasted_iota(jnp.int32, square, 1) < lax.broadcasted_iota(jnp.int32, square, 0)
        for copy in lists:
            copy.wait()
        owners = jnp.concatenate(
            [owner_ref[:, r * BLOCK:(r + 1) * BLOCK] for r in range(lines)]
            + [jnp.full((16 - lines, BLOCK), -1, jnp.int32)], axis=0)
        named = jnp.concatenate([(owners == o).astype(f32) for o in range(N_OWNER)], axis=0)
        named_16 = named.astype(bf16)
        along = jnp.dot(named_16, up_to.astype(f32).astype(bf16), preferred_element_type=f32)
        line_sums = jnp.dot(named_16, jnp.ones(square, bf16), preferred_element_type=f32)
        before = jnp.dot(below.astype(f32).astype(bf16), line_sums.astype(bf16), preferred_element_type=f32)
        spot = jnp.sum((named * (before + along - 1.0)).reshape(N_OWNER, -1, BLOCK), axis=0)
        starts_v[...] = before.reshape(N_OWNER, -1, BLOCK)[:, 0].astype(jnp.int32)
        spot_t = jnp.pad(spot, ((0, BLOCK - spot.shape[0]), (0, 0))).T
        wide = (BLOCK, 2 * BLOCK)
        place = lax.broadcasted_iota(jnp.int32, wide, 1)
        chip_of, pos, chunk = place & (CHIPS - 1), lax.shift_right_logical(place, 4) & 3, lax.shift_right_logical(place, 6)
        wanted = (CHIPS * (24 * pos + CHUNKS * z + chunk) + chip_of).astype(f32)
        which = lax.broadcasted_iota(jnp.int32, (8, BLOCK), 0)
        found = jnp.zeros((8, 2 * BLOCK), f32)
        for r in range(lines):
            hit = jnp.where(spot_t[:, r:r + 1] == wanted, 1.0, 0.0).astype(bf16)
            value = jnp.where(which == 0, row_ref[r:r + 1, :], col_ref[r:r + 1, :]).astype(f32).astype(bf16)
            found = found + jnp.dot(value, hit, preferred_element_type=f32)
        spots_v[...] = found.astype(jnp.int32)
        copies = [pltpu.make_async_copy(spots_v, spots, load_sem.at[2]),
                  pltpu.make_async_copy(starts_v, starts, load_sem.at[3])]
        for copy in copies:
            copy.start()
        for copy in copies:
            copy.wait()

    early = hidden.shape[0] // 2
    lax.fori_loop(0, early, load_hidden, 0, unroll=8)
    make_places()
    pltpu.make_async_copy(grad, grad, load_sem.at[0]).wait()

    def turn(k, carry):
        for n in range(2):
            load(hidden_hbm, hidden, load_sem.at[1], early + 2 * k + n)
        grad_t[k] = grad[k].T
        return carry

    late = hidden.shape[0] - early
    lax.fori_loop(0, late // 2, turn, 0, unroll=4)

    def turn_only(k, carry):
        grad_t[k] = grad[k].T
        return carry

    lax.fori_loop(late // 2, grad.shape[0], turn_only, 0, unroll=4)
    pltpu.make_async_copy(hidden, hidden, load_sem.at[1]).wait()
    states = [pltpu.make_async_copy(src, dst, load_sem.at[4 + n]) for n, (src, dst) in enumerate(
        ((master_hbm, master), (moment1_hbm, moment1), (moment2_hbm, moment2)))]
    for state in states:
        state.start()

    def send(src, dst, item, kind, who):
        pltpu.make_async_remote_copy(
            src_ref=src, dst_ref=dst, send_sem=send_sem.at[kind], recv_sem=recv_sem.at[item, kind],
            device_id=who, device_id_type=MESH).start()

    def take(ref, sem):
        pltpu.make_async_copy(ref, ref, sem).wait()

    def arrive(ref, item, kind):
        take(ref.at[item], recv_sem.at[item, kind])

    def product(place):
        row = jnp.clip(spots[0, place], 0, hidden.shape[0] - 1)
        col = jnp.clip(spots[1, place], 0, grad_t.shape[0] - 1)
        return jnp.dot(grad_t[col], hidden[row], preferred_element_type=f32)

    def slot_of(item, ra, rb, core):
        if item % 2 == 0:
            px, py = wrap(x + ra, 4), wrap(y + rb, 4)
        else:
            px, py = wrap(x + rb, 4), wrap(y + ra, 4)
        return ((item // 2) * 4 + 2 * core + item % 2) * CHIPS + px * 4 + py

    def partner_products(item):
        for j in range(CHIPS):
            to_pair[item, j] = product(slot_of(item, j // 4, j % 4, 1 - c)).astype(bf16)
        if item == int(ORDER[0][1]):
            pl.semaphore_wait(barrier, len(everyone))
        send(to_pair.at[item], from_pair.at[item], item, PAIR, partner)

    def own_products(item):
        arrive(from_pair, item, PAIR)

        for j in range(CHIPS):
            value = product(slot_of(item, j // 4, j % 4, c)) + from_pair[item, j].astype(f32)
            chip[item, j] = value.astype(bf16)

    def ring_start(item):
        axis = item % 2
        send(chip.at[item, pl.ds(8, 2)], ring_a.at[item, 0], item, XA, near(axis, 1))
        send(chip.at[item, pl.ds(10, 2)], ring_a.at[item, 1], item, XA, near(axis, 3))

    def ring_own(item):
        axis = item % 2
        send(chip.at[item, pl.ds(6, 2)], ring_b.at[item, 0, pl.ds(2, 2)], item, XB, near(axis, 1))
        send(chip.at[item, pl.ds(12, 2)], ring_b.at[item, 1, pl.ds(0, 2)], item, XB, near(axis, 3))

    def ring_step(item):
        axis = item % 2
        arrive(ring_a, item, XA)
        chip[item, 4:6] = (chip[item, 4:6].astype(f32) + ring_a[item, 0].astype(f32)).astype(bf16)
        send(chip.at[item, pl.ds(4, 2)], ring_b.at[item, 0, pl.ds(0, 2)], item, XB, near(axis, 1))
        chip[item, 14:16] = (chip[item, 14:16].astype(f32) + ring_a[item, 1].astype(f32)).astype(bf16)
        send(chip.at[item, pl.ds(14, 2)], ring_b.at[item, 1, pl.ds(2, 2)], item, XB, near(axis, 3))

    def ring_end(item):
        axis = 1 - item % 2
        arrive(ring_b, item, XB)
        for rb in (2, 1, 3, 0):
            value = (chip[item, rb].astype(f32) + ring_b[item, 0, rb].astype(f32)
                     + ring_b[item, 1, rb].astype(f32))
            line[item, rb] = value.astype(bf16)
        for step in (2, 1, 3):
            send(line.at[item, step], last.at[item, step - 1], item, YA, near(axis, step))

    def finish(item):
        arrive(last, item, YA)
        value = line[item, 0].astype(f32)
        for k in range(3):
            value = value + last[item, k].astype(f32)
        done[item // 2][c * 2 + item % 2] = value.T.astype(bf16)
        return jnp.sum(value * value, axis=0, keepdims=True)

    done = (done_0, done_1, done_2)
    me_chip = x * 4 + y
    half = BLOCK // 2
    mine = pl.ds(pl.multiple_of(c * half, half), half)

    def move(src, dst, kind, index, who):
        pltpu.make_async_remote_copy(
            src_ref=src, dst_ref=dst, send_sem=move_send.at[kind + index], recv_sem=move_recv.at[kind + index],
            device_id=who, device_id_type=MESH).start()

    def share_done(chunk):
        move(done[chunk].at[pl.ds(2 * c, 2)], done[chunk].at[pl.ds(2 * c, 2)], DONE, chunk, partner)

    def held_for(chunk, owner):
        first = jnp.clip(starts[owner, 0], 0, listed) - me_chip - CHIPS * (CHUNKS * z + chunk) + 383
        pos = jnp.minimum(lax.div(jnp.maximum(first, 0), 384), 3)
        return done[chunk][pos]

    def to_owners(chunk):
        take(done[chunk].at[pl.ds(2 - 2 * c, 2)], move_recv.at[DONE + chunk])
        for j in (1, 2, 0):
            owner = wrap(z + 2 * j + 1 + c, N_OWNER)
            to_owner[chunk, j] = held_for(chunk, owner)
            move(to_owner.at[chunk, j], gathered.at[chunk * 8 + c * 3 + j], OWNER, chunk, {"owner": owner})
        owner = wrap(z + 7, N_OWNER)
        to_owner[chunk, 3] = held_for(chunk, owner)
        move(to_owner.at[chunk, 3, mine], gathered.at[chunk * 8 + 6, mine], OWNER, chunk, {"owner": owner})
        gathered[chunk * 8 + 7] = held_for(chunk, z)

    def share_gathered(chunk):
        take(size_ref, move_recv.at[OWNER + chunk])
        trio = gathered.at[pl.ds(chunk * 8 + c * 3, 3)]
        move(trio, trio, GATHER, chunk, partner)
        rest = gathered.at[chunk * 8 + 6, mine]
        move(rest, rest, GATHER, chunk, partner)

    start = jnp.clip(starts[z, 0], 0, listed)
    count = jnp.where(z == N_OWNER - 1, listed, starts[jnp.minimum(z + 1, N_OWNER - 1), 0]) - start

    def block_for(to_chip):
        first = start + share * (2 * to_chip + c)
        spot = first + ((me_chip - first) & (CHIPS - 1))
        q = jnp.minimum(lax.div(spot, CHIPS), 95)
        chunk = wrap(q, CHUNKS)
        away = (z - lax.div(q, CHUNKS)) & (N_OWNER - 1)
        index = 3 * ((away + 1) & 1) + lax.shift_right_logical(away + 7, 1) - 4
        index = jnp.where(away == 0, 7, jnp.where(away == 7, 6, index))
        return gathered[chunk * 8 + index]

    def to_slots():
        for chunk in range(CHUNKS):
            take(size_ref, move_recv.at[GATHER + chunk])
        for k in sorted(range(len(offsets)), key=lambda k: -sum(min(v, 4 - v) for v in offsets[k])):
            dx, dy = offsets[k]
            to_slot[k] = block_for(wrap(x + dx, 4) * 4 + wrap(y + dy, 4))
            move(to_slot.at[k], landed.at[me_chip], SLOT, 0, spread[k])
        landed[me_chip] = block_for(me_chip)

    def decay_states():
        for state in states:
            state.wait()
        for i in range(share):
            master[i] = (1.0 - 0.25 * 0.1) * master[i]
            moment1[i] = 0.9 * moment1[i]
            moment2[i] = 0.95 * moment2[i]

    def store_slots(total):
        clip = 1.0 / jnp.maximum(jnp.sqrt(jnp.full((BLOCK, BLOCK), total, f32)), 1.0)
        take(to_slot, move_recv.at[SLOT])
        for i in range(share):
            slot = d * share + i
            value = landed[(start + slot) & (CHIPS - 1)].astype(f32)
            scaled = clip * (value * (slot < count).astype(f32))
            first = moment1[i] + 0.1 * scaled
            second = moment2[i] + 0.05 * scaled * scaled
            root = jnp.sqrt(second * (1.0 / (1.0 - 0.95**10))) + 1e-08
            updated_ref[i] = master[i] - first * (0.25 / (1.0 - 0.9**10)) / root

    def add_start(n, value):
        first = sum(len(group) for group in groups[:n])
        sums[n] = value
        for k, who in enumerate(groups[n]):
            pltpu.make_async_remote_copy(
                src_ref=sums.at[n], dst_ref=sum_in.at[first + k], send_sem=sum_send.at[0],
                recv_sem=sum_recv.at[n], device_id=who, device_id_type=MESH).start()
        return n, first

    def add_end(value, adding):
        n, first = adding
        size = len(groups[n])
        take(sum_in.at[pl.ds(first, size)], sum_recv.at[n])
        for k in range(size):
            value = value + sum_in[first + k]
        return value

    def close(item):
        parts.append(finish(item))

    parts, adding = [], []

    def add_next():
        value = adding[-1][0] if adding else functools.reduce(jnp.add, parts)
        if adding:
            value = add_end(value, adding[-1][1])
        n = len(adding)
        if n < len(groups):
            adding.append((value, add_start(n, value)))
        return value

    stages = {"P": partner_products, "O": own_products, "A": ring_start, "B": ring_own, "R": ring_step, "E": ring_end,
              "F": close, "s": share_done, "z": to_owners, "g": share_gathered, "a": lambda _: add_next()}
    for name, index in zip("".join(ORDER)[::2], "".join(ORDER)[1::2]):
        stages[name](int(index))
    to_slots()
    decay_states()
    total = jnp.sum(add_next())
    store_slots(total)
    for kind, ref in ((PAIR, to_pair), (XA, ring_a), (XB, ring_b), (YA, last)):
        take(ref, send_sem.at[kind])
    for chunk in range(CHUNKS):
        take(done[chunk].at[pl.ds(0, 2)], move_send.at[DONE + chunk])
        take(size_ref, move_send.at[OWNER + chunk])
        take(size_ref, move_send.at[GATHER + chunk])
    take(to_slot, move_send.at[SLOT])
    take(sum_in, sum_send.at[0])


def step(block_row, block_col, owner_of, hidden, grad_out, master, moment1, moment2):
    share = master.shape[0]
    listed = block_row.shape[0]
    tokens, features = hidden.shape[0], grad_out.shape[1]
    bf16, f32 = jnp.bfloat16, jnp.float32
    items = 2 * CHUNKS
    peers = 1 + CHIPS - 1 + N_OWNER - 1
    block = (BLOCK, BLOCK)
    vmem = pl.BlockSpec(memory_space=pltpu.VMEM)
    hbm = pl.BlockSpec(memory_space=pltpu.HBM)
    return pl.pallas_call(
        functools.partial(kernel, items, share, listed),
        out_shape=jax.ShapeDtypeStruct((share, *block), f32),
        in_specs=[hbm] * 8,
        out_specs=vmem,
        scratch_shapes=[
            pltpu.VMEM((share, *block), f32),
            pltpu.VMEM((share, *block), f32),
            pltpu.VMEM((share, *block), f32),
            pltpu.VMEM((listed // BLOCK, BLOCK), jnp.int32),
            pltpu.VMEM((listed // BLOCK, BLOCK), jnp.int32),
            pltpu.VMEM((1, listed), jnp.int32),
            pltpu.VMEM((7 * BLOCK // 2, BLOCK), bf16),
            pltpu.VMEM((8, 2 * BLOCK), jnp.int32),
            pltpu.VMEM((N_OWNER, BLOCK), jnp.int32),
            pltpu.SMEM((8, 2 * BLOCK), jnp.int32),
            pltpu.SMEM((N_OWNER, BLOCK), jnp.int32),
            pltpu.VMEM((hidden.shape[1] // BLOCK, tokens, BLOCK), bf16),
            pltpu.VMEM((features // BLOCK, tokens, BLOCK), bf16),
            pltpu.VMEM((features // BLOCK, BLOCK, tokens), bf16),
            pltpu.VMEM((items, 16, *block), bf16),
            pltpu.VMEM((items, 16, *block), bf16),
            pltpu.VMEM((items, 16, *block), bf16),
            pltpu.VMEM((items, 2, 2, *block), bf16),
            pltpu.VMEM((items, 2, 4, *block), bf16),
            pltpu.VMEM((items, 4, *block), bf16),
            pltpu.VMEM((items, 3, *block), bf16),
            pltpu.VMEM((4, *block), bf16),
            pltpu.VMEM((4, *block), bf16),
            pltpu.VMEM((4, *block), bf16),
            pltpu.VMEM((CHUNKS, 4, *block), bf16),
            pltpu.VMEM((CHUNKS * N_OWNER, *block), bf16),
            pltpu.VMEM((CHIPS - 1, *block), bf16),
            pltpu.VMEM((CHIPS, *block), bf16),
            pltpu.VMEM((3, 1, BLOCK), f32),
            pltpu.VMEM((peers, 1, BLOCK), f32),
            pltpu.SemaphoreType.DMA((10,)),
            pltpu.SemaphoreType.DMA((4,)),
            pltpu.SemaphoreType.DMA((items, 4)),
            pltpu.SemaphoreType.DMA((10,)),
            pltpu.SemaphoreType.DMA((10,)),
            pltpu.SemaphoreType.DMA((1,)),
            pltpu.SemaphoreType.DMA((3,)),
        ],
        compiler_params=pltpu.CompilerParams(
            collective_id=0, has_side_effects=True, vmem_limit_bytes=36 * 1024 * 1024),
        name="step",
    )(*[pltpu.with_memory_space_constraint(x, pltpu.HBM) for x in (
        block_row.reshape(-1, BLOCK), block_col.reshape(-1, BLOCK), owner_of.T, hidden, grad_out,
        master, moment1, moment2)])


def on_device(hidden, grad_out, block_row, block_col, owner_of, master, moment1, moment2):
    updated = step(block_row, block_col, owner_of, hidden, grad_out, master[0], moment1[0], moment2[0])
    return updated[None]


def solution(mesh):
    placed = (
        P("dp", None),
        P("dp", None),
        P(),
        P(),
        P(),
        P("owner", "dp", None, None),
        P("owner", "dp", None, None),
        P("owner", "dp", None, None),
    )
    return jax.shard_map(
        on_device,
        mesh=mesh,
        in_specs=placed,
        out_specs=P("owner", "dp", None, None),
        check_vma=False,
    )
```

```python
import functools

import jax
import jax.numpy as jnp
from jax import lax
from jax.experimental import pallas as pl
from jax.experimental.pallas import tpu as pltpu
from jax.sharding import PartitionSpec as P

BLOCK = 128
N_OWNER = 8
MESH = pl.DeviceIdType.MESH
CHUNKS = 3
ORDER = (
    "P0P1P5P2P4O0A0B0O1A1B1O5P3A5O4O2A2R0A4R1O3A3B3R2E1B2E0",
    "R3B4R5B5R4E2E3F0F1s0z0E4E5F3F2s1z1F5F4s2a0z2a0g0g1a0g2",
)
CHIPS = 16
PAIR, XA, XB, YA = range(4)
DONE, OWNER, GATHER, SLOT = 0, 3, 6, 9


def wrap(value, size):
    return lax.rem(value, size)


def kernel(items, share, listed, row_hbm, col_hbm, owner_hbm, hidden_hbm, grad_hbm,
           master_hbm, moment1_hbm, moment2_hbm, updated_ref, master, moment1, moment2,
           row_ref, col_ref, owner_ref, size_ref, spots_v, starts_v, spots, starts, hidden, grad, grad_t, to_pair, from_pair, chip, ring_a, ring_b, line, last,
           done_0, done_1, done_2, to_owner, gathered, to_slot, landed,
           sums, sum_in, load_sem, send_sem, recv_sem, move_send, move_recv, sum_send, sum_recv):
    f32, bf16 = jnp.float32, jnp.bfloat16
    d = lax.axis_index("dp")
    z = lax.axis_index("owner")
    x, y, c = lax.div(d, 8), wrap(lax.div(d, 2), 4), wrap(d, 2)

    def device(px, py, pc):
        return {"dp": (px * 4 + py) * 2 + pc}

    partner = device(x, y, 1 - c)

    def near(axis, step):
        if axis == 0:
            return device(wrap(x + step, 4), y, c)
        return device(x, wrap(y + step, 4), c)

    lists = [pltpu.make_async_copy(src, dst, load_sem.at[7 + n]) for n, (src, dst) in enumerate(
        ((owner_hbm, owner_ref), (row_hbm, row_ref), (col_hbm, col_ref)))]
    for copy in lists:
        copy.start()

    barrier = pltpu.get_barrier_semaphore()
    offsets = [(dx, dy) for dx in range(4) for dy in range(4) if dx or dy]
    spread = [device(wrap(x + dx, 4), wrap(y + dy, 4), c) for dx, dy in offsets]
    groups = [[partner], spread, [{"owner": wrap(z + k, N_OWNER)} for k in range(1, N_OWNER)]]
    everyone = sum(groups, [])
    for who in everyone:
        pl.semaphore_signal(barrier, inc=1, device_id=who, device_id_type=MESH)

    def load(src, dst, sem, k):
        columns = pl.ds(pl.multiple_of(k * BLOCK, BLOCK), BLOCK)
        pltpu.make_async_copy(src.at[:, columns], dst.at[k], sem).start()

    def load_grad(k, carry):
        load(grad_hbm, grad, load_sem.at[0], k)
        return carry

    lax.fori_loop(0, grad.shape[0], load_grad, 0, unroll=8)

    def load_hidden(k, carry):
        load(hidden_hbm, hidden, load_sem.at[1], k)
        return carry

    def make_places():
        square = (BLOCK, BLOCK)
        lines = listed // BLOCK
        up_to = lax.broadcasted_iota(jnp.int32, square, 0) <= lax.broadcasted_iota(jnp.int32, square, 1)
        below = lax.broadcasted_iota(jnp.int32, square, 1) < lax.broadcasted_iota(jnp.int32, square, 0)
        for copy in lists:
            copy.wait()
        owners = jnp.concatenate(
            [owner_ref[:, r * BLOCK:(r + 1) * BLOCK] for r in range(lines)]
            + [jnp.full((16 - lines, BLOCK), -1, jnp.int32)], axis=0)
        named = jnp.concatenate([(owners == o).astype(f32) for o in range(N_OWNER)], axis=0)
        named_16 = named.astype(bf16)
        along = jnp.dot(named_16, up_to.astype(f32).astype(bf16), preferred_element_type=f32)
        line_sums = jnp.dot(named_16, jnp.ones(square, bf16), preferred_element_type=f32)
        before = jnp.dot(below.astype(f32).astype(bf16), line_sums.astype(bf16), preferred_element_type=f32)
        spot = jnp.sum((named * (before + along - 1.0)).reshape(N_OWNER, -1, BLOCK), axis=0)
        starts_v[...] = before.reshape(N_OWNER, -1, BLOCK)[:, 0].astype(jnp.int32)
        spot_t = jnp.pad(spot, ((0, BLOCK - spot.shape[0]), (0, 0))).T
        wide = (BLOCK, 2 * BLOCK)
        place = lax.broadcasted_iota(jnp.int32, wide, 1)
        chip_of, pos, chunk = place & (CHIPS - 1), lax.shift_right_logical(place, 4) & 3, lax.shift_right_logical(place, 6)
        wanted = (CHIPS * (24 * pos + CHUNKS * z + chunk) + chip_of).astype(f32)
        which = lax.broadcasted_iota(jnp.int32, (8, BLOCK), 0)
        found = jnp.zeros((8, 2 * BLOCK), f32)
        for r in range(lines):
            hit = jnp.where(spot_t[:, r:r + 1] == wanted, 1.0, 0.0).astype(bf16)
            value = jnp.where(which == 0, row_ref[r:r + 1, :], col_ref[r:r + 1, :]).astype(f32).astype(bf16)
            found = found + jnp.dot(value, hit, preferred_element_type=f32)
        spots_v[...] = found.astype(jnp.int32)
        copies = [pltpu.make_async_copy(spots_v, spots, load_sem.at[2]),
                  pltpu.make_async_copy(starts_v, starts, load_sem.at[3])]
        for copy in copies:
            copy.start()
        for copy in copies:
            copy.wait()

    early = hidden.shape[0] // 2
    lax.fori_loop(0, early, load_hidden, 0, unroll=8)
    make_places()
    pltpu.make_async_copy(grad, grad, load_sem.at[0]).wait()

    def turn(k, carry):
        for n in range(2):
            load(hidden_hbm, hidden, load_sem.at[1], early + 2 * k + n)
        grad_t[k] = grad[k].T
        return carry

    late = hidden.shape[0] - early
    lax.fori_loop(0, late // 2, turn, 0, unroll=4)

    def turn_only(k, carry):
        grad_t[k] = grad[k].T
        return carry

    lax.fori_loop(late // 2, grad.shape[0], turn_only, 0, unroll=4)
    pltpu.make_async_copy(hidden, hidden, load_sem.at[1]).wait()
    states = [pltpu.make_async_copy(src, dst, load_sem.at[4 + n]) for n, (src, dst) in enumerate(
        ((master_hbm, master), (moment1_hbm, moment1), (moment2_hbm, moment2)))]
    for state in states:
        state.start()

    def send(src, dst, item, kind, who):
        pltpu.make_async_remote_copy(
            src_ref=src, dst_ref=dst, send_sem=send_sem.at[kind], recv_sem=recv_sem.at[item, kind],
            device_id=who, device_id_type=MESH).start()

    def take(ref, sem):
        pltpu.make_async_copy(ref, ref, sem).wait()

    def arrive(ref, item, kind):
        take(ref.at[item], recv_sem.at[item, kind])

    def product(place):
        row = jnp.clip(spots[0, place], 0, hidden.shape[0] - 1)
        col = jnp.clip(spots[1, place], 0, grad_t.shape[0] - 1)
        return jnp.dot(grad_t[col], hidden[row], preferred_element_type=f32)

    def slot_of(item, ra, rb, core):
        if item % 2 == 0:
            px, py = wrap(x + ra, 4), wrap(y + rb, 4)
        else:
            px, py = wrap(x + rb, 4), wrap(y + ra, 4)
        return ((item // 2) * 4 + 2 * core + item % 2) * CHIPS + px * 4 + py

    def partner_products(item):
        for j in range(CHIPS):
            to_pair[item, j] = product(slot_of(item, j // 4, j % 4, 1 - c)).astype(bf16)
        if item == int(ORDER[0][1]):
            pl.semaphore_wait(barrier, len(everyone))
        send(to_pair.at[item], from_pair.at[item], item, PAIR, partner)

    def own_products(item):
        arrive(from_pair, item, PAIR)

        for j in range(CHIPS):
            value = product(slot_of(item, j // 4, j % 4, c)) + from_pair[item, j].astype(f32)
            chip[item, j] = value.astype(bf16)

    def ring_start(item):
        axis = item % 2
        send(chip.at[item, pl.ds(8, 2)], ring_a.at[item, 0], item, XA, near(axis, 1))
        send(chip.at[item, pl.ds(10, 2)], ring_a.at[item, 1], item, XA, near(axis, 3))

    def ring_own(item):
        axis = item % 2
        send(chip.at[item, pl.ds(6, 2)], ring_b.at[item, 0, pl.ds(2, 2)], item, XB, near(axis, 1))
        send(chip.at[item, pl.ds(12, 2)], ring_b.at[item, 1, pl.ds(0, 2)], item, XB, near(axis, 3))

    def ring_step(item):
        axis = item % 2
        arrive(ring_a, item, XA)
        chip[item, 4:6] = (chip[item, 4:6].astype(f32) + ring_a[item, 0].astype(f32)).astype(bf16)
        send(chip.at[item, pl.ds(4, 2)], ring_b.at[item, 0, pl.ds(0, 2)], item, XB, near(axis, 1))
        chip[item, 14:16] = (chip[item, 14:16].astype(f32) + ring_a[item, 1].astype(f32)).astype(bf16)
        send(chip.at[item, pl.ds(14, 2)], ring_b.at[item, 1, pl.ds(2, 2)], item, XB, near(axis, 3))

    def ring_end(item):
        axis = 1 - item % 2
        arrive(ring_b, item, XB)
        for rb in (2, 1, 3, 0):
            value = (chip[item, rb].astype(f32) + ring_b[item, 0, rb].astype(f32)
                     + ring_b[item, 1, rb].astype(f32))
            line[item, rb] = value.astype(bf16)
        for step in (2, 1, 3):
            send(line.at[item, step], last.at[item, step - 1], item, YA, near(axis, step))

    def finish(item):
        arrive(last, item, YA)
        value = line[item, 0].astype(f32)
        for k in range(3):
            value = value + last[item, k].astype(f32)
        done[item // 2][c * 2 + item % 2] = value.T.astype(bf16)
        return jnp.sum(value * value, axis=0, keepdims=True)

    done = (done_0, done_1, done_2)
    me_chip = x * 4 + y
    half = BLOCK // 2
    mine = pl.ds(pl.multiple_of(c * half, half), half)

    def move(src, dst, kind, index, who):
        pltpu.make_async_remote_copy(
            src_ref=src, dst_ref=dst, send_sem=move_send.at[kind + index], recv_sem=move_recv.at[kind + index],
            device_id=who, device_id_type=MESH).start()

    def share_done(chunk):
        move(done[chunk].at[pl.ds(2 * c, 2)], done[chunk].at[pl.ds(2 * c, 2)], DONE, chunk, partner)

    def held_for(chunk, owner):
        first = jnp.clip(starts[owner, 0], 0, listed) - me_chip - CHIPS * (CHUNKS * z + chunk) + 383
        pos = jnp.minimum(lax.div(jnp.maximum(first, 0), 384), 3)
        return done[chunk][pos]

    def to_owners(chunk):
        take(done[chunk].at[pl.ds(2 - 2 * c, 2)], move_recv.at[DONE + chunk])
        for j in (1, 2, 0):
            owner = wrap(z + 2 * j + 1 + c, N_OWNER)
            to_owner[chunk, j] = held_for(chunk, owner)
            move(to_owner.at[chunk, j], gathered.at[chunk * 8 + c * 3 + j], OWNER, chunk, {"owner": owner})
        owner = wrap(z + 7, N_OWNER)
        to_owner[chunk, 3] = held_for(chunk, owner)
        move(to_owner.at[chunk, 3, mine], gathered.at[chunk * 8 + 6, mine], OWNER, chunk, {"owner": owner})
        gathered[chunk * 8 + 7] = held_for(chunk, z)

    def share_gathered(chunk):
        take(size_ref, move_recv.at[OWNER + chunk])
        trio = gathered.at[pl.ds(chunk * 8 + c * 3, 3)]
        move(trio, trio, GATHER, chunk, partner)
        rest = gathered.at[chunk * 8 + 6, mine]
        move(rest, rest, GATHER, chunk, partner)

    start = jnp.clip(starts[z, 0], 0, listed)
    count = jnp.where(z == N_OWNER - 1, listed, starts[jnp.minimum(z + 1, N_OWNER - 1), 0]) - start

    def block_for(to_chip):
        first = start + share * (2 * to_chip + c)
        spot = first + ((me_chip - first) & (CHIPS - 1))
        q = jnp.minimum(lax.div(spot, CHIPS), 95)
        chunk = wrap(q, CHUNKS)
        away = (z - lax.div(q, CHUNKS)) & (N_OWNER - 1)
        index = 3 * ((away + 1) & 1) + lax.shift_right_logical(away + 7, 1) - 4
        index = jnp.where(away == 0, 7, jnp.where(away == 7, 6, index))
        return gathered[chunk * 8 + index]

    def to_slots():
        for chunk in range(CHUNKS):
            take(size_ref, move_recv.at[GATHER + chunk])
        for k in sorted(range(len(offsets)), key=lambda k: -sum(min(v, 4 - v) for v in offsets[k])):
            dx, dy = offsets[k]
            to_slot[k] = block_for(wrap(x + dx, 4) * 4 + wrap(y + dy, 4))
            move(to_slot.at[k], landed.at[me_chip], SLOT, 0, spread[k])
        landed[me_chip] = block_for(me_chip)

    def decay_states():
        for state in states:
            state.wait()
        for i in range(share):
            master[i] = (1.0 - 0.25 * 0.1) * master[i]
            moment1[i] = 0.9 * moment1[i]
            moment2[i] = 0.95 * moment2[i]

    def store_slots(total):
        clip = 1.0 / jnp.maximum(jnp.sqrt(jnp.full((BLOCK, BLOCK), total, f32)), 1.0)
        take(to_slot, move_recv.at[SLOT])
        for i in range(share):
            slot = d * share + i
            value = landed[(start + slot) & (CHIPS - 1)].astype(f32)
            scaled = clip * (value * (slot < count).astype(f32))
            first = moment1[i] + 0.1 * scaled
            second = moment2[i] + 0.05 * scaled * scaled
            root = jnp.sqrt(second * (1.0 / (1.0 - 0.95**10))) + 1e-08
            updated_ref[i] = master[i] - first * (0.25 / (1.0 - 0.9**10)) / root

    def add_start(n, value):
        first = sum(len(group) for group in groups[:n])
        sums[n] = value
        for k, who in enumerate(groups[n]):
            pltpu.make_async_remote_copy(
                src_ref=sums.at[n], dst_ref=sum_in.at[first + k], send_sem=sum_send.at[0],
                recv_sem=sum_recv.at[n], device_id=who, device_id_type=MESH).start()
        return n, first

    def add_end(value, adding):
        n, first = adding
        size = len(groups[n])
        take(sum_in.at[pl.ds(first, size)], sum_recv.at[n])
        for k in range(size):
            value = value + sum_in[first + k]
        return value

    def close(item):
        parts.append(finish(item))

    parts, adding = [], []

    def add_next():
        value = adding[-1][0] if adding else functools.reduce(jnp.add, parts)
        if adding:
            value = add_end(value, adding[-1][1])
        n = len(adding)
        if n < len(groups):
            adding.append((value, add_start(n, value)))
        return value

    stages = {"P": partner_products, "O": own_products, "A": ring_start, "B": ring_own, "R": ring_step, "E": ring_end,
              "F": close, "s": share_done, "z": to_owners, "g": share_gathered, "a": lambda _: add_next()}
    for name, index in zip("".join(ORDER)[::2], "".join(ORDER)[1::2]):
        stages[name](int(index))
    to_slots()
    decay_states()
    total = jnp.sum(add_next())
    store_slots(total)
    for kind, ref in ((PAIR, to_pair), (XA, ring_a), (XB, ring_b), (YA, last)):
        take(ref, send_sem.at[kind])
    for chunk in range(CHUNKS):
        take(done[chunk].at[pl.ds(0, 2)], move_send.at[DONE + chunk])
        take(size_ref, move_send.at[OWNER + chunk])
        take(size_ref, move_send.at[GATHER + chunk])
    take(to_slot, move_send.at[SLOT])
    take(sum_in, sum_send.at[0])


def step(block_row, block_col, owner_of, hidden, grad_out, master, moment1, moment2):
    share = master.shape[0]
    listed = block_row.shape[0]
    tokens, features = hidden.shape[0], grad_out.shape[1]
    bf16, f32 = jnp.bfloat16, jnp.float32
    items = 2 * CHUNKS
    peers = 1 + CHIPS - 1 + N_OWNER - 1
    block = (BLOCK, BLOCK)
    vmem = pl.BlockSpec(memory_space=pltpu.VMEM)
    hbm = pl.BlockSpec(memory_space=pltpu.HBM)
    return pl.pallas_call(
        functools.partial(kernel, items, share, listed),
        out_shape=jax.ShapeDtypeStruct((share, *block), f32),
        in_specs=[hbm] * 8,
        out_specs=vmem,
        scratch_shapes=[
            pltpu.VMEM((share, *block), f32),
            pltpu.VMEM((share, *block), f32),
            pltpu.VMEM((share, *block), f32),
            pltpu.VMEM((listed // BLOCK, BLOCK), jnp.int32),
            pltpu.VMEM((listed // BLOCK, BLOCK), jnp.int32),
            pltpu.VMEM((1, listed), jnp.int32),
            pltpu.VMEM((7 * BLOCK // 2, BLOCK), bf16),
            pltpu.VMEM((8, 2 * BLOCK), jnp.int32),
            pltpu.VMEM((N_OWNER, BLOCK), jnp.int32),
            pltpu.SMEM((8, 2 * BLOCK), jnp.int32),
            pltpu.SMEM((N_OWNER, BLOCK), jnp.int32),
            pltpu.VMEM((hidden.shape[1] // BLOCK, tokens, BLOCK), bf16),
            pltpu.VMEM((features // BLOCK, tokens, BLOCK), bf16),
            pltpu.VMEM((features // BLOCK, BLOCK, tokens), bf16),
            pltpu.VMEM((items, 16, *block), bf16),
            pltpu.VMEM((items, 16, *block), bf16),
            pltpu.VMEM((items, 16, *block), bf16),
            pltpu.VMEM((items, 2, 2, *block), bf16),
            pltpu.VMEM((items, 2, 4, *block), bf16),
            pltpu.VMEM((items, 4, *block), bf16),
            pltpu.VMEM((items, 3, *block), bf16),
            pltpu.VMEM((4, *block), bf16),
            pltpu.VMEM((4, *block), bf16),
            pltpu.VMEM((4, *block), bf16),
            pltpu.VMEM((CHUNKS, 4, *block), bf16),
            pltpu.VMEM((CHUNKS * N_OWNER, *block), bf16),
            pltpu.VMEM((CHIPS - 1, *block), bf16),
            pltpu.VMEM((CHIPS, *block), bf16),
            pltpu.VMEM((3, 1, BLOCK), f32),
            pltpu.VMEM((peers, 1, BLOCK), f32),
            pltpu.SemaphoreType.DMA((10,)),
            pltpu.SemaphoreType.DMA((4,)),
            pltpu.SemaphoreType.DMA((items, 4)),
            pltpu.SemaphoreType.DMA((10,)),
            pltpu.SemaphoreType.DMA((10,)),
            pltpu.SemaphoreType.DMA((1,)),
            pltpu.SemaphoreType.DMA((3,)),
        ],
        compiler_params=pltpu.CompilerParams(
            collective_id=0, has_side_effects=True, vmem_limit_bytes=36 * 1024 * 1024),
        name="step",
    )(*[pltpu.with_memory_space_constraint(x, pltpu.HBM) for x in (
        block_row.reshape(-1, BLOCK), block_col.reshape(-1, BLOCK), owner_of.T, hidden, grad_out,
        master, moment1, moment2)])


def on_device(hidden, grad_out, block_row, block_col, owner_of, master, moment1, moment2):
    updated = step(block_row, block_col, owner_of, hidden, grad_out, master[0], moment1[0], moment2[0])
    return updated[None]


def solution(mesh):
    placed = (
        P("dp", None),
        P("dp", None),
        P(),
        P(),
        P(),
        P("owner", "dp", None, None),
        P("owner", "dp", None, None),
        P("owner", "dp", None, None),
    )
    return jax.shard_map(
        on_device,
        mesh=mesh,
        in_specs=placed,
        out_specs=P("owner", "dp", None, None),
        check_vma=False,
    )
```

```python
import functools

import jax
import jax.numpy as jnp
from jax import lax
from jax.experimental import pallas as pl
from jax.experimental.pallas import tpu as pltpu
from jax.sharding import PartitionSpec as P

BLOCK = 128
N_OWNER = 8
MESH = pl.DeviceIdType.MESH
CHUNKS = 3
ORDER = (
    "P0P1P5P2P4O0O1O5P3A5O4O2A2R0A4R1O3A3B3R2E1B2E0",
    "R3B4R5B5R4E2E3F0F1s0z0E4E5F3F2s1z1F5F4s2a0z2a0g0g1a0g2",
)
CHIPS = 16
PAIR, XA, XB, YA = range(4)
DONE, OWNER, GATHER, SLOT = 0, 3, 6, 9


def wrap(value, size):
    return lax.rem(value, size)


def kernel(items, share, listed, row_hbm, col_hbm, owner_hbm, hidden_hbm, grad_hbm,
           master_hbm, moment1_hbm, moment2_hbm, updated_ref, master, moment1, moment2,
           row_ref, col_ref, owner_ref, size_ref, spots_v, starts_v, spots, starts, hidden, grad, grad_t, to_pair, from_pair, chip, ring_a, ring_b, line, last,
           done_0, done_1, done_2, to_owner, gathered, to_slot, landed,
           sums, sum_in, load_sem, send_sem, recv_sem, move_send, move_recv, sum_send, sum_recv):
    f32, bf16 = jnp.float32, jnp.bfloat16
    d = lax.axis_index("dp")
    z = lax.axis_index("owner")
    x, y, c = lax.div(d, 8), wrap(lax.div(d, 2), 4), wrap(d, 2)

    def device(px, py, pc):
        return {"dp": (px * 4 + py) * 2 + pc}

    partner = device(x, y, 1 - c)

    def near(axis, step):
        if axis == 0:
            return device(wrap(x + step, 4), y, c)
        return device(x, wrap(y + step, 4), c)

    lists = [pltpu.make_async_copy(src, dst, load_sem.at[7 + n]) for n, (src, dst) in enumerate(
        ((owner_hbm, owner_ref), (row_hbm, row_ref), (col_hbm, col_ref)))]
    for copy in lists:
        copy.start()

    barrier = pltpu.get_barrier_semaphore()
    offsets = [(dx, dy) for dx in range(4) for dy in range(4) if dx or dy]
    spread = [device(wrap(x + dx, 4), wrap(y + dy, 4), c) for dx, dy in offsets]
    groups = [[partner], spread, [{"owner": wrap(z + k, N_OWNER)} for k in range(1, N_OWNER)]]
    everyone = sum(groups, [])
    for who in everyone:
        pl.semaphore_signal(barrier, inc=1, device_id=who, device_id_type=MESH)

    def load(src, dst, sem, k):
        columns = pl.ds(pl.multiple_of(k * BLOCK, BLOCK), BLOCK)
        pltpu.make_async_copy(src.at[:, columns], dst.at[k], sem).start()

    def load_grad(k, carry):
        load(grad_hbm, grad, load_sem.at[0], k)
        return carry

    lax.fori_loop(0, grad.shape[0], load_grad, 0, unroll=8)

    def load_hidden(k, carry):
        load(hidden_hbm, hidden, load_sem.at[1], k)
        return carry

    def make_places():
        square = (BLOCK, BLOCK)
        lines = listed // BLOCK
        up_to = lax.broadcasted_iota(jnp.int32, square, 0) <= lax.broadcasted_iota(jnp.int32, square, 1)
        below = lax.broadcasted_iota(jnp.int32, square, 1) < lax.broadcasted_iota(jnp.int32, square, 0)
        for copy in lists:
            copy.wait()
        owners = jnp.concatenate(
            [owner_ref[:, r * BLOCK:(r + 1) * BLOCK] for r in range(lines)]
            + [jnp.full((16 - lines, BLOCK), -1, jnp.int32)], axis=0)
        named = jnp.concatenate([(owners == o).astype(f32) for o in range(N_OWNER)], axis=0)
        named_16 = named.astype(bf16)
        along = jnp.dot(named_16, up_to.astype(f32).astype(bf16), preferred_element_type=f32)
        line_sums = jnp.dot(named_16, jnp.ones(square, bf16), preferred_element_type=f32)
        before = jnp.dot(below.astype(f32).astype(bf16), line_sums.astype(bf16), preferred_element_type=f32)
        spot = jnp.sum((named * (before + along - 1.0)).reshape(N_OWNER, -1, BLOCK), axis=0)
        starts_v[...] = before.reshape(N_OWNER, -1, BLOCK)[:, 0].astype(jnp.int32)
        spot_t = jnp.pad(spot, ((0, BLOCK - spot.shape[0]), (0, 0))).T
        wide = (BLOCK, 2 * BLOCK)
        place = lax.broadcasted_iota(jnp.int32, wide, 1)
        chip_of, pos, chunk = place & (CHIPS - 1), lax.shift_right_logical(place, 4) & 3, lax.shift_right_logical(place, 6)
        wanted = (CHIPS * (24 * pos + CHUNKS * z + chunk) + chip_of).astype(f32)
        which = lax.broadcasted_iota(jnp.int32, (8, BLOCK), 0)
        found = jnp.zeros((8, 2 * BLOCK), f32)
        for r in range(lines):
            hit = jnp.where(spot_t[:, r:r + 1] == wanted, 1.0, 0.0).astype(bf16)
            value = jnp.where(which == 0, row_ref[r:r + 1, :], col_ref[r:r + 1, :]).astype(f32).astype(bf16)
            found = found + jnp.dot(value, hit, preferred_element_type=f32)
        spots_v[...] = found.astype(jnp.int32)
        copies = [pltpu.make_async_copy(spots_v, spots, load_sem.at[2]),
                  pltpu.make_async_copy(starts_v, starts, load_sem.at[3])]
        for copy in copies:
            copy.start()
        for copy in copies:
            copy.wait()

    early = hidden.shape[0] // 2
    lax.fori_loop(0, early, load_hidden, 0, unroll=8)
    make_places()
    pltpu.make_async_copy(grad, grad, load_sem.at[0]).wait()

    def turn(k, carry):
        for n in range(2):
            load(hidden_hbm, hidden, load_sem.at[1], early + 2 * k + n)
        grad_t[k] = grad[k].T
        return carry

    late = hidden.shape[0] - early
    lax.fori_loop(0, late // 2, turn, 0, unroll=4)

    def turn_only(k, carry):
        grad_t[k] = grad[k].T
        return carry

    lax.fori_loop(late // 2, grad.shape[0], turn_only, 0, unroll=4)
    pltpu.make_async_copy(hidden, hidden, load_sem.at[1]).wait()
    states = [pltpu.make_async_copy(src, dst, load_sem.at[4 + n]) for n, (src, dst) in enumerate(
        ((master_hbm, master), (moment1_hbm, moment1), (moment2_hbm, moment2)))]
    for state in states:
        state.start()

    def send(src, dst, item, kind, who):
        pltpu.make_async_remote_copy(
            src_ref=src, dst_ref=dst, send_sem=send_sem.at[kind], recv_sem=recv_sem.at[item, kind],
            device_id=who, device_id_type=MESH).start()

    def take(ref, sem):
        pltpu.make_async_copy(ref, ref, sem).wait()

    def arrive(ref, item, kind):
        take(ref.at[item], recv_sem.at[item, kind])

    def product(place):
        row = jnp.clip(spots[0, place], 0, hidden.shape[0] - 1)
        col = jnp.clip(spots[1, place], 0, grad_t.shape[0] - 1)
        return jnp.dot(grad_t[col], hidden[row], preferred_element_type=f32)

    def slot_of(item, ra, rb, core):
        if item % 2 == 0:
            px, py = wrap(x + ra, 4), wrap(y + rb, 4)
        else:
            px, py = wrap(x + rb, 4), wrap(y + ra, 4)
        return ((item // 2) * 4 + 2 * core + item % 2) * CHIPS + px * 4 + py

    def partner_products(item):
        for j in range(CHIPS):
            to_pair[item, j] = product(slot_of(item, j // 4, j % 4, 1 - c)).astype(bf16)
        if item == int(ORDER[0][1]):
            pl.semaphore_wait(barrier, len(everyone))
        send(to_pair.at[item], from_pair.at[item], item, PAIR, partner)

    def own_products(item):
        arrive(from_pair, item, PAIR)

        for n, j in enumerate((8, 9, 10, 11, 6, 7, 12, 13, 4, 5, 14, 15, 0, 1, 2, 3)):
            value = product(slot_of(item, j // 4, j % 4, c)) + from_pair[item, j].astype(f32)
            chip[item, j] = value.astype(bf16)
            if item < 2 and n == 3:
                ring_start(item)
            if item < 2 and n == 7:
                ring_own(item)

    def ring_start(item):
        axis = item % 2
        send(chip.at[item, pl.ds(8, 2)], ring_a.at[item, 0], item, XA, near(axis, 1))
        send(chip.at[item, pl.ds(10, 2)], ring_a.at[item, 1], item, XA, near(axis, 3))

    def ring_own(item):
        axis = item % 2
        send(chip.at[item, pl.ds(6, 2)], ring_b.at[item, 0, pl.ds(2, 2)], item, XB, near(axis, 1))
        send(chip.at[item, pl.ds(12, 2)], ring_b.at[item, 1, pl.ds(0, 2)], item, XB, near(axis, 3))

    def ring_step(item):
        axis = item % 2
        arrive(ring_a, item, XA)
        chip[item, 4:6] = (chip[item, 4:6].astype(f32) + ring_a[item, 0].astype(f32)).astype(bf16)
        send(chip.at[item, pl.ds(4, 2)], ring_b.at[item, 0, pl.ds(0, 2)], item, XB, near(axis, 1))
        chip[item, 14:16] = (chip[item, 14:16].astype(f32) + ring_a[item, 1].astype(f32)).astype(bf16)
        send(chip.at[item, pl.ds(14, 2)], ring_b.at[item, 1, pl.ds(2, 2)], item, XB, near(axis, 3))

    def ring_end(item):
        axis = 1 - item % 2
        arrive(ring_b, item, XB)
        for rb in (2, 1, 3, 0):
            value = (chip[item, rb].astype(f32) + ring_b[item, 0, rb].astype(f32)
                     + ring_b[item, 1, rb].astype(f32))
            line[item, rb] = value.astype(bf16)
        for step in (2, 1, 3):
            send(line.at[item, step], last.at[item, step - 1], item, YA, near(axis, step))

    def finish(item):
        arrive(last, item, YA)
        value = line[item, 0].astype(f32)
        for k in range(3):
            value = value + last[item, k].astype(f32)
        done[item // 2][c * 2 + item % 2] = value.T.astype(bf16)
        return jnp.sum(value * value, axis=0, keepdims=True)

    done = (done_0, done_1, done_2)
    me_chip = x * 4 + y
    half = BLOCK // 2
    mine = pl.ds(pl.multiple_of(c * half, half), half)

    def move(src, dst, kind, index, who):
        pltpu.make_async_remote_copy(
            src_ref=src, dst_ref=dst, send_sem=move_send.at[kind + index], recv_sem=move_recv.at[kind + index],
            device_id=who, device_id_type=MESH).start()

    def share_done(chunk):
        move(done[chunk].at[pl.ds(2 * c, 2)], done[chunk].at[pl.ds(2 * c, 2)], DONE, chunk, partner)

    def held_for(chunk, owner):
        first = jnp.clip(starts[owner, 0], 0, listed) - me_chip - CHIPS * (CHUNKS * z + chunk) + 383
        pos = jnp.minimum(lax.div(jnp.maximum(first, 0), 384), 3)
        return done[chunk][pos]

    def to_owners(chunk):
        take(done[chunk].at[pl.ds(2 - 2 * c, 2)], move_recv.at[DONE + chunk])
        for j in (1, 2, 0):
            owner = wrap(z + 2 * j + 1 + c, N_OWNER)
            to_owner[chunk, j] = held_for(chunk, owner)
            move(to_owner.at[chunk, j], gathered.at[chunk * 8 + c * 3 + j], OWNER, chunk, {"owner": owner})
        owner = wrap(z + 7, N_OWNER)
        to_owner[chunk, 3] = held_for(chunk, owner)
        move(to_owner.at[chunk, 3, mine], gathered.at[chunk * 8 + 6, mine], OWNER, chunk, {"owner": owner})
        gathered[chunk * 8 + 7] = held_for(chunk, z)

    def share_gathered(chunk):
        take(size_ref, move_recv.at[OWNER + chunk])
        trio = gathered.at[pl.ds(chunk * 8 + c * 3, 3)]
        move(trio, trio, GATHER, chunk, partner)
        rest = gathered.at[chunk * 8 + 6, mine]
        move(rest, rest, GATHER, chunk, partner)

    start = jnp.clip(starts[z, 0], 0, listed)
    count = jnp.where(z == N_OWNER - 1, listed, starts[jnp.minimum(z + 1, N_OWNER - 1), 0]) - start

    def block_for(to_chip):
        first = start + share * (2 * to_chip + c)
        spot = first + ((me_chip - first) & (CHIPS - 1))
        q = jnp.minimum(lax.div(spot, CHIPS), 95)
        chunk = wrap(q, CHUNKS)
        away = (z - lax.div(q, CHUNKS)) & (N_OWNER - 1)
        index = 3 * ((away + 1) & 1) + lax.shift_right_logical(away + 7, 1) - 4
        index = jnp.where(away == 0, 7, jnp.where(away == 7, 6, index))
        return gathered[chunk * 8 + index]

    def to_slots():
        for chunk in range(CHUNKS):
            take(size_ref, move_recv.at[GATHER + chunk])
        for k in sorted(range(len(offsets)), key=lambda k: -sum(min(v, 4 - v) for v in offsets[k])):
            dx, dy = offsets[k]
            to_slot[k] = block_for(wrap(x + dx, 4) * 4 + wrap(y + dy, 4))
            move(to_slot.at[k], landed.at[me_chip], SLOT, 0, spread[k])
        landed[me_chip] = block_for(me_chip)

    def decay_states():
        for state in states:
            state.wait()
        for i in range(share):
            master[i] = (1.0 - 0.25 * 0.1) * master[i]
            moment1[i] = 0.9 * moment1[i]
            moment2[i] = 0.95 * moment2[i]

    def store_slots(total):
        clip = 1.0 / jnp.maximum(jnp.sqrt(jnp.full((BLOCK, BLOCK), total, f32)), 1.0)
        take(to_slot, move_recv.at[SLOT])
        for i in range(share):
            slot = d * share + i
            value = landed[(start + slot) & (CHIPS - 1)].astype(f32)
            scaled = clip * (value * (slot < count).astype(f32))
            first = moment1[i] + 0.1 * scaled
            second = moment2[i] + 0.05 * scaled * scaled
            root = jnp.sqrt(second * (1.0 / (1.0 - 0.95**10))) + 1e-08
            updated_ref[i] = master[i] - first * (0.25 / (1.0 - 0.9**10)) / root

    def add_start(n, value):
        first = sum(len(group) for group in groups[:n])
        sums[n] = value
        for k, who in enumerate(groups[n]):
            pltpu.make_async_remote_copy(
                src_ref=sums.at[n], dst_ref=sum_in.at[first + k], send_sem=sum_send.at[0],
                recv_sem=sum_recv.at[n], device_id=who, device_id_type=MESH).start()
        return n, first

    def add_end(value, adding):
        n, first = adding
        size = len(groups[n])
        take(sum_in.at[pl.ds(first, size)], sum_recv.at[n])
        for k in range(size):
            value = value + sum_in[first + k]
        return value

    def close(item):
        parts.append(finish(item))

    parts, adding = [], []

    def add_next():
        value = adding[-1][0] if adding else functools.reduce(jnp.add, parts)
        if adding:
            value = add_end(value, adding[-1][1])
        n = len(adding)
        if n < len(groups):
            adding.append((value, add_start(n, value)))
        return value

    stages = {"P": partner_products, "O": own_products, "A": ring_start, "B": ring_own, "R": ring_step, "E": ring_end,
              "F": close, "s": share_done, "z": to_owners, "g": share_gathered, "a": lambda _: add_next()}
    for name, index in zip("".join(ORDER)[::2], "".join(ORDER)[1::2]):
        stages[name](int(index))
    to_slots()
    decay_states()
    total = jnp.sum(add_next())
    store_slots(total)
    for kind, ref in ((PAIR, to_pair), (XA, ring_a), (XB, ring_b), (YA, last)):
        take(ref, send_sem.at[kind])
    for chunk in range(CHUNKS):
        take(done[chunk].at[pl.ds(0, 2)], move_send.at[DONE + chunk])
        take(size_ref, move_send.at[OWNER + chunk])
        take(size_ref, move_send.at[GATHER + chunk])
    take(to_slot, move_send.at[SLOT])
    take(sum_in, sum_send.at[0])


def step(block_row, block_col, owner_of, hidden, grad_out, master, moment1, moment2):
    share = master.shape[0]
    listed = block_row.shape[0]
    tokens, features = hidden.shape[0], grad_out.shape[1]
    bf16, f32 = jnp.bfloat16, jnp.float32
    items = 2 * CHUNKS
    peers = 1 + CHIPS - 1 + N_OWNER - 1
    block = (BLOCK, BLOCK)
    vmem = pl.BlockSpec(memory_space=pltpu.VMEM)
    hbm = pl.BlockSpec(memory_space=pltpu.HBM)
    return pl.pallas_call(
        functools.partial(kernel, items, share, listed),
        out_shape=jax.ShapeDtypeStruct((share, *block), f32),
        in_specs=[hbm] * 8,
        out_specs=vmem,
        scratch_shapes=[
            pltpu.VMEM((share, *block), f32),
            pltpu.VMEM((share, *block), f32),
            pltpu.VMEM((share, *block), f32),
            pltpu.VMEM((listed // BLOCK, BLOCK), jnp.int32),
            pltpu.VMEM((listed // BLOCK, BLOCK), jnp.int32),
            pltpu.VMEM((1, listed), jnp.int32),
            pltpu.VMEM((7 * BLOCK // 2, BLOCK), bf16),
            pltpu.VMEM((8, 2 * BLOCK), jnp.int32),
            pltpu.VMEM((N_OWNER, BLOCK), jnp.int32),
            pltpu.SMEM((8, 2 * BLOCK), jnp.int32),
            pltpu.SMEM((N_OWNER, BLOCK), jnp.int32),
            pltpu.VMEM((hidden.shape[1] // BLOCK, tokens, BLOCK), bf16),
            pltpu.VMEM((features // BLOCK, tokens, BLOCK), bf16),
            pltpu.VMEM((features // BLOCK, BLOCK, tokens), bf16),
            pltpu.VMEM((items, 16, *block), bf16),
            pltpu.VMEM((items, 16, *block), bf16),
            pltpu.VMEM((items, 16, *block), bf16),
            pltpu.VMEM((items, 2, 2, *block), bf16),
            pltpu.VMEM((items, 2, 4, *block), bf16),
            pltpu.VMEM((items, 4, *block), bf16),
            pltpu.VMEM((items, 3, *block), bf16),
            pltpu.VMEM((4, *block), bf16),
            pltpu.VMEM((4, *block), bf16),
            pltpu.VMEM((4, *block), bf16),
            pltpu.VMEM((CHUNKS, 4, *block), bf16),
            pltpu.VMEM((CHUNKS * N_OWNER, *block), bf16),
            pltpu.VMEM((CHIPS - 1, *block), bf16),
            pltpu.VMEM((CHIPS, *block), bf16),
            pltpu.VMEM((3, 1, BLOCK), f32),
            pltpu.VMEM((peers, 1, BLOCK), f32),
            pltpu.SemaphoreType.DMA((10,)),
            pltpu.SemaphoreType.DMA((4,)),
            pltpu.SemaphoreType.DMA((items, 4)),
            pltpu.SemaphoreType.DMA((10,)),
            pltpu.SemaphoreType.DMA((10,)),
            pltpu.SemaphoreType.DMA((1,)),
            pltpu.SemaphoreType.DMA((3,)),
        ],
        compiler_params=pltpu.CompilerParams(
            collective_id=0, has_side_effects=True, vmem_limit_bytes=36 * 1024 * 1024),
        name="step",
    )(*[pltpu.with_memory_space_constraint(x, pltpu.HBM) for x in (
        block_row.reshape(-1, BLOCK), block_col.reshape(-1, BLOCK), owner_of.T, hidden, grad_out,
        master, moment1, moment2)])


def on_device(hidden, grad_out, block_row, block_col, owner_of, master, moment1, moment2):
    updated = step(block_row, block_col, owner_of, hidden, grad_out, master[0], moment1[0], moment2[0])
    return updated[None]


def solution(mesh):
    placed = (
        P("dp", None),
        P("dp", None),
        P(),
        P(),
        P(),
        P("owner", "dp", None, None),
        P("owner", "dp", None, None),
        P("owner", "dp", None, None),
    )
    return jax.shard_map(
        on_device,
        mesh=mesh,
        in_specs=placed,
        out_specs=P("owner", "dp", None, None),
        check_vma=False,
    )
```
